128 devices in a mesh: dp: 8 (over y, core), row: 4 (over z), col: 4 (over x).
Axes of the slice: x: 4, y: 4, z: 4, core: 2. Of those that a mesh axis runs over, the one named last changes fastest.
Arguments:
- inputs: bfloat16 [8, 256, 128, 512], P('dp', None, 'row', 'col'), may hold values from -6 to 6
- reduce_weight: bfloat16 [64, 256], replicated, may hold values from -0.375 to 0.375
- spatial_weight: bfloat16 [3, 3, 64, 64], replicated, may hold values from -0.25 to 0.25
- expand_weight: bfloat16 [256, 64], replicated, may hold values from -0.75 to 0.75
- class_weight: bfloat16 [3, 3, 135, 256], replicated, may hold values from -0.125 to 0.125
- anchor_labels: int32 [8, 9, 128, 512], P('dp', None, 'row', 'col'), may hold values from 0 to 15, as said below
- anchor_mask: int32 [8, 9, 128, 512], P('dp', None, 'row', 'col'), may hold values from 0 to 1, as said below
Outputs:
- loss: float32 [], replicated
- grad_reduce: float32 [64, 256], replicated
- grad_spatial: float32 [3, 3, 64, 64], replicated
- grad_expand: float32 [256, 64], replicated
- grad_class: float32 [3, 3, 135, 256], replicated
The draws below stay inside these ranges and needn't reach their ends.
Inputs may be any that keep to these rules, and one draw needn't show every extreme that they name: `anchor_labels`: labels are 0 to 15; anchor 0 at the first row and column of every tile is positive. `anchor_mask`: every anchor with a label above 0 has mask 1.
All inputs are finite; a program needn't handle non-finite values.
Results may differ from the reference program's by a relative error of at most 0.0034.
Values may be sent and summed in bfloat16 or wider, within the bound.
No kernel may reach another device: no remote copies, remote signals or barrier semaphores. Data moves between devices by JAX's collectives and lax.ppermute only.
A program may use at most 128 MiB of HBM per device.

```python
import jax
import jax.numpy as jnp
from jax import lax

C = 256
MID = 64
A = 9
K = 15
TILES = 8
H = 128
W = 512


def anchor_pair(key):
    label_key = jax.random.fold_in(key, 11)
    class_key = jax.random.fold_in(key, 12)
    valid_key = jax.random.fold_in(key, 13)
    shape = (TILES, A, H, W)
    tile_index = jnp.arange(TILES, dtype=jnp.int32)[:, None, None, None]
    row_index = jnp.arange(H, dtype=jnp.int32)[None, None, :, None]
    place = tile_index * H + row_index
    threshold = 10 + 20 * place // max(TILES * H - 1, 1)
    rolled = jax.random.randint(label_key, shape, 0, 1000, dtype=jnp.int32)
    classes = jax.random.randint(class_key, shape, 1, K + 1, dtype=jnp.int32)
    labels = jnp.where(rolled < threshold, classes, 0)
    anchor_index = jnp.arange(A, dtype=jnp.int32)[None, :, None, None]
    column_index = jnp.arange(W, dtype=jnp.int32)[None, None, None, :]
    forced = (anchor_index == 0) & (row_index == 0) & (column_index == 0)
    labels = jnp.where(forced, jnp.maximum(classes, 1), labels)
    valid = jax.random.randint(valid_key, shape, 0, 100, dtype=jnp.int32) < 85
    mask = jnp.where((labels > 0) | valid, 1, 0).astype(jnp.int32)
    return (labels.astype(jnp.int32), mask)


def draw_anchor_labels(key, part):
    return anchor_pair(key)[0]


def draw_anchor_mask(key, part):
    return anchor_pair(key)[1]


def levels(key, extent, split, smallest, top_value):
    level = 1.0
    for axis_at, blocks in split:
        steps = jax.random.uniform(jax.random.fold_in(jax.random.fold_in(key, 6), axis_at), (blocks,), jnp.float32, smallest / len(split), top_value / len(split))
        level = level * jnp.repeat(jnp.exp(steps), extent[axis_at] // blocks).reshape((-1,) + (1,) * (len(extent) - 1 - axis_at))
    return level


def scatter_about(key, shape, width, bound, shards=(), kind=jnp.bfloat16):
    entries = width * jax.random.normal(key, shape, jnp.float32)
    if shards:
        entries = entries * levels(key, shape, shards, -0.22, 0.18)
    return jnp.clip(entries, -bound, bound).astype(kind)


def setup_inputs(seed: int = 0) -> dict:
    arg_keys = jax.random.split(jax.random.key(seed), 8)
    inputs = scatter_about(arg_keys[0], (TILES, C, H, W), 1.0, 6.0, ((0, 8), (2, 4), (3, 4)))
    reduce_weight = scatter_about(arg_keys[1], (MID, C), C ** -0.5, 0.375)
    spatial_weight = scatter_about(arg_keys[2], (3, 3, MID, MID), (9 * MID) ** -0.5, 0.25)
    expand_weight = scatter_about(arg_keys[3], (C, MID), MID ** -0.5, 0.75)
    class_weight = scatter_about(arg_keys[4], (3, 3, A * K, C), (9 * C) ** -0.5, 0.125)
    anchor_labels = draw_anchor_labels(jax.random.fold_in(arg_keys[7], 71), 0)
    anchor_mask = draw_anchor_mask(jax.random.fold_in(arg_keys[7], 71), 0)
    return dict(inputs=inputs, reduce_weight=reduce_weight, spatial_weight=spatial_weight, expand_weight=expand_weight, class_weight=class_weight, anchor_labels=anchor_labels, anchor_mask=anchor_mask)


def conv_three(padded, weight, rows, cols):
    total = jnp.zeros((padded.shape[0], weight.shape[2], rows, cols), jnp.float32)
    for dy in range(3):
        for dx in range(3):
            total = total + jnp.einsum('oc,bchw->bohw', weight[dy, dx].astype(jnp.float32), padded[:, :, dy:dy + rows, dx:dx + cols].astype(jnp.float32), precision=lax.Precision.HIGHEST)
    return total

def weight_three(dout, padded, rows, cols):
    taps = []
    for dy in range(3):
        for dx in range(3):
            taps.append(jnp.einsum('bohw,bchw->oc', dout.astype(jnp.float32), padded[:, :, dy:dy + rows, dx:dx + cols].astype(jnp.float32), precision=lax.Precision.HIGHEST))
    return jnp.stack(taps).reshape(3, 3, taps[0].shape[0], taps[0].shape[1])

def input_three(dout_pad, weight, rows, cols):
    total = jnp.zeros((dout_pad.shape[0], weight.shape[3], rows, cols), jnp.float32)
    for ey in range(3):
        for ex in range(3):
            total = total + jnp.einsum('oc,bohw->bchw', weight[2 - ey, 2 - ex].astype(jnp.float32), dout_pad[:, :, ey:ey + rows, ex:ex + cols].astype(jnp.float32), precision=lax.Precision.HIGHEST)
    return total

def focal_terms(logits, labels, mask):
    shaped = logits.reshape(logits.shape[0], A, K, logits.shape[2], logits.shape[3])
    classes = jnp.arange(1, K + 1, dtype=jnp.int32)[None, None, :, None, None]
    target = labels[:, :, None] == classes
    signs = jnp.where(target, 1.0, -1.0).astype(shaped.dtype)
    alpha = jnp.where(target, 0.25, 0.75).astype(shaped.dtype)
    terms = -alpha * jax.nn.sigmoid(-signs * shaped) ** 2 * jax.nn.log_sigmoid(signs * shaped)
    return jnp.sum(terms * mask[:, :, None].astype(shaped.dtype))

def pad_cells(field):
    return jnp.pad(field, ((0, 0), (0, 0), (1, 1), (1, 1)))

def one_tile(inputs, labels, mask, reduce_weight, spatial_weight, expand_weight, class_weight):
    rows, cols = (inputs.shape[2], inputs.shape[3])
    first = jax.nn.relu(jnp.einsum('mc,bchw->bmhw', reduce_weight.astype(jnp.float32), inputs.astype(jnp.float32), precision=lax.Precision.HIGHEST)).astype(jnp.bfloat16)
    first_pad = pad_cells(first)
    second = jax.nn.relu(conv_three(first_pad, spatial_weight, rows, cols)).astype(jnp.bfloat16)
    block = jax.nn.relu(inputs.astype(jnp.float32) + jnp.einsum('cm,bmhw->bchw', expand_weight.astype(jnp.float32), second.astype(jnp.float32), precision=lax.Precision.HIGHEST)).astype(jnp.bfloat16)
    block_pad = pad_cells(block)
    logits = conv_three(block_pad, class_weight, rows, cols)
    focal, pullback = jax.vjp(lambda z: focal_terms(z, labels, mask), logits)
    dlogits = pullback(jnp.ones_like(focal))[0].astype(jnp.bfloat16)
    count = jnp.sum((labels > 0).astype(jnp.float32))
    class_sum = weight_three(dlogits, block_pad, rows, cols)
    dblock = input_three(pad_cells(dlogits), class_weight, rows, cols)
    dsum = jnp.where(block > 0, dblock, 0.0).astype(jnp.bfloat16)
    expand_sum = jnp.einsum('bchw,bmhw->cm', dsum.astype(jnp.float32), second.astype(jnp.float32), precision=lax.Precision.HIGHEST)
    dsecond = jnp.where(second > 0, jnp.einsum('cm,bchw->bmhw', expand_weight.astype(jnp.float32), dsum.astype(jnp.float32), precision=lax.Precision.HIGHEST), 0.0).astype(jnp.bfloat16)
    spatial_sum = weight_three(dsecond, first_pad, rows, cols)
    dfirst = jnp.where(first > 0, input_three(pad_cells(dsecond), spatial_weight, rows, cols), 0.0).astype(jnp.bfloat16)
    reduce_sum = jnp.einsum('bmhw,bchw->mc', dfirst.astype(jnp.float32), inputs.astype(jnp.float32), precision=lax.Precision.HIGHEST)
    return (reduce_sum, spatial_sum, expand_sum, class_sum, focal, count)

def reference(inputs, reduce_weight, spatial_weight, expand_weight, class_weight, anchor_labels, anchor_mask):

    def per_tile(items):
        return one_tile(items[0][None], items[1][None], items[2][None], reduce_weight, spatial_weight, expand_weight, class_weight)
    results = lax.map(per_tile, (inputs, anchor_labels, anchor_mask))
    summed = [lax.optimization_barrier(jnp.sum(item, axis=0)) for item in results]
    positives = summed[5]
    loss = summed[4] / positives
    return (loss, summed[0] / positives, summed[1] / positives, summed[2] / positives, summed[3] / positives)
```

```python
import jax
import jax.numpy as jnp
import numpy as np
from jax import lax
from jax.experimental import pallas as pl
from jax.experimental.pallas import tpu as pltpu
from jax.sharding import PartitionSpec as P

A = 9
K = 15
OUT = A * K
C = 256
MID = 64
HALO = 4
ROWS = 32
COLS = 128
FULL = ROWS + 2 * HALO
STRIDE = COLS + 2 * HALO
CHANNELS = 288
MARGIN = 256
WIDTH = 6400
CHUNK = 512
LABEL0 = C
MASK0 = C + A
ONE0 = C + 2 * A
TAIL = 8
STACK = 9 * 128 + 9 * TAIL + 8
ALL = ("dp", "row", "col")
TAPS = [(dy - 1) * STRIDE + (dx - 1) for dy in range(3) for dx in range(3)]
BF = jnp.bfloat16
F32 = jnp.float32


def row_of(top_ref, main_ref, bottom_ref, r):
    if r < HALO:
        return top_ref[r]
    if r < HALO + ROWS:
        return main_ref[r - HALO]
    return bottom_ref[r - HALO - ROWS]


def lanes_between(lo, hi):
    lane = lax.broadcasted_iota(jnp.int32, (CHANNELS, 128), 1)
    return (lane >= lo) & (lane < hi)


def put(ref, tile, value, lo, hi):
    where = slice(tile * 128, tile * 128 + 128)
    ref[:, where] = jnp.where(lanes_between(lo, hi), value, ref[:, where])


def pack_kernel(main_ref, top_ref, bottom_ref, left_ref, right_ref):
    left_ref[...] = jnp.zeros_like(left_ref)
    right_ref[...] = jnp.zeros_like(right_ref)
    for r in range(FULL):
        row = row_of(top_ref, main_ref, bottom_ref, r)
        at = (4 * r) % 128
        put(left_ref, 4 * r // 128, pltpu.roll(row, at, 1), at, at + 4)
        put(right_ref, 4 * r // 128, pltpu.roll(row, (at + 4) % 128, 1), at, at + 4)


def window(ref, rows, lane, shift):
    base = (shift // 128) * 128
    turn = shift - base
    if turn == 0:
        return ref[rows, pl.ds(pl.multiple_of(lane + base, 128), CHUNK)]
    wide = ref[rows, pl.ds(pl.multiple_of(lane + base, 128), CHUNK + 128)]
    return pltpu.roll(wide, CHUNK + 128 - turn, 1)[:, :CHUNK]


def interior(lane, shift):
    p = lane - MARGIN + shift + lax.broadcasted_iota(jnp.int32, (1, CHUNK), 1)
    r = (p * 30841) >> 22
    c = p - r * STRIDE
    return (r >= HALO) & (r < HALO + ROWS) & (c >= HALO) & (c < HALO + COLS)


def dot(a, b):
    return jnp.dot(a, b, preferred_element_type=F32)


def dot_nt(a, b):
    return lax.dot_general(a, b, (((1,), (1,)), ((), ())), preferred_element_type=F32)


def chunks(start, count, body):
    def step(j, carry):
        body(pl.multiple_of(MARGIN + start + j * CHUNK, 128))
        return carry

    lax.fori_loop(0, count, step, 0)


def main_kernel(
    main_ref, top_ref, bottom_ref, left_ref, right_ref,
    wr_ref, w2_ref, w2t_ref, we_ref, wet_ref, w3_ref, w3t_ref, e_ref,
    gclass_ref, gred_ref, gspat_ref, gexp_ref, stat_ref,
    x_ref, first_ref, second_ref, block_ref, d_ref, dt_ref, ds_ref, facc_ref, cacc_ref,
):
    for ref in (x_ref, first_ref, second_ref, block_ref, d_ref, dt_ref, ds_ref):
        ref[...] = jnp.zeros_like(ref)
    for ref in (gclass_ref, gred_ref, gspat_ref, gexp_ref, facc_ref, cacc_ref):
        ref[...] = jnp.zeros_like(ref)
    for r in range(FULL):
        row = row_of(top_ref, main_ref, bottom_ref, r)
        at = MARGIN + r * STRIDE + HALO
        turn, tile = (at % 128, at // 128)
        turned = pltpu.roll(row, turn, 1)
        put(x_ref, tile, turned, turn, 128)
        put(x_ref, tile + 1, turned, 0, turn)
        source = slice(4 * r // 128 * 128, 4 * r // 128 * 128 + 128)
        at = MARGIN + r * STRIDE
        put(x_ref, at // 128, pltpu.roll(left_ref[:, source], (4 * r) % 128, 1), at % 128, at % 128 + 4)
        at = at + HALO + COLS
        put(x_ref, at // 128, pltpu.roll(right_ref[:, source], (4 * r + 4) % 128, 1), at % 128, at % 128 + 4)

    def first_step(lane):
        x = x_ref[:C, pl.ds(lane, CHUNK)]
        first_ref[:, pl.ds(lane, CHUNK)] = jnp.maximum(dot(wr_ref[...], x), 0.0).astype(BF)

    chunks(0, 11, first_step)

    def block_step(lane):
        here = pl.ds(lane, CHUNK)
        stack = jnp.concatenate([window(first_ref, slice(None), lane, s) for s in TAPS], axis=0)
        second = jnp.maximum(dot(w2_ref[...], stack), 0.0)
        inside = x_ref[ONE0 - 2 : ONE0 + 14, here].astype(F32)[2:3]
        second = jnp.where(inside > 0.5, second, 0.0).astype(BF)
        second_ref[:, here] = second
        total = x_ref[:C, here].astype(F32) + dot(we_ref[...], second)
        block_ref[:, here] = jnp.maximum(total, 0.0).astype(BF)

    chunks(128, 11, block_step)

    channel = lax.broadcasted_iota(jnp.int32, (136, 1), 0)
    wanted = (channel - 15 * ((channel * 4370) >> 16) + 17).astype(F32)

    def logit_step(lane):
        here = pl.ds(lane, CHUNK)
        stack = jnp.concatenate([window(block_ref, slice(None), lane, s) for s in TAPS], axis=0)
        z = dot(w3_ref[...], stack)
        tags = x_ref[C:CHANNELS, here]
        code = dot(e_ref[...], tags)
        target = code == wanted
        counted = code > 15.5
        u = jnp.where(target, z, -z)
        alpha = jnp.where(target, 0.25, 0.75)
        e = jnp.exp(-jnp.abs(u))
        d = 1.0 / (1.0 + e)
        ed = e * d
        positive = u >= 0
        p = jnp.where(positive, ed, d)
        q = jnp.where(positive, d, ed)
        ls = jnp.minimum(u, 0.0) - jnp.log1p(e)
        ap2 = jnp.where(counted, alpha, 0.0) * p * p
        grad = ap2 * (2.0 * q * ls - p)
        grad = jnp.where(target, grad, -grad)
        d_ref[:, here] = grad[:128].astype(BF)
        dt_ref[:, here] = grad[128:].astype(BF).astype(F32)
        inner = interior(lane, 0)
        focal = jnp.where(inner, ap2 * ls, 0.0)
        facc_ref[...] -= jnp.sum(focal.reshape(17, 8, CHUNK), axis=0)
        labels = tags[:16].astype(F32)
        tag = lax.broadcasted_iota(jnp.int32, (16, CHUNK), 0)
        positives = jnp.where((labels > 0.5) & (tag < A) & inner, 1.0, 0.0)
        cacc_ref[...] += positives[:8] + positives[8:]

    chunks(256, 10, logit_step)

    def class_step(lane):
        here = pl.ds(lane, CHUNK)
        mains = [window(d_ref, slice(None), lane, -s) for s in TAPS]
        tails = [window(dt_ref, slice(None), lane, -s) for s in TAPS]
        inner = [interior(lane, -s) for s in TAPS]
        spare = jnp.zeros((8, CHUNK), F32)
        block = block_ref[:, here]
        stack = jnp.concatenate(
            mains + [jnp.concatenate(tails + [spare], axis=0).astype(BF)], axis=0
        )
        dblock = dot(w3t_ref[...], stack)
        dsum = jnp.where(block.astype(F32) > 0, dblock, 0.0).astype(BF)
        second = second_ref[:, here]
        within = interior(lane, 0)
        second32 = second.astype(F32)
        gexp_ref[...] += dot_nt(dsum, jnp.where(within, second32, 0.0).astype(BF))
        ds_ref[:, here] = jnp.where(second32 > 0, dot(wet_ref[...], dsum), 0.0).astype(BF)
        own = jnp.concatenate(
            [m * jnp.where(i, 1.0, 0.0).astype(BF) for m, i in zip(mains, inner)]
            + [
                jnp.concatenate(
                    [jnp.where(i, t, 0.0) for t, i in zip(tails, inner)] + [spare], axis=0
                ).astype(BF)
            ],
            axis=0,
        )
        gclass_ref[...] += dot_nt(own, block)

    chunks(384, 10, class_step)

    def first_back(lane):
        here = pl.ds(lane, CHUNK)
        parts = [window(ds_ref, slice(None), lane, -s) for s in TAPS]
        inner = [interior(lane, -s) for s in TAPS]
        first = first_ref[:, here]
        own = jnp.concatenate(
            [m * jnp.where(i, 1.0, 0.0).astype(BF) for m, i in zip(parts, inner)], axis=0
        )
        gspat_ref[...] += dot_nt(own, first)
        dfirst = dot(w2t_ref[...], jnp.concatenate(parts, axis=0))
        keep = (first.astype(F32) > 0) & interior(lane, 0)
        dfirst = jnp.where(keep, dfirst, 0.0).astype(BF)
        gred_ref[...] += dot_nt(dfirst, x_ref[:C, here])

    chunks(384, 10, first_back)

    focal = jnp.sum(facc_ref[...])
    count = jnp.sum(cacc_ref[...])
    lane = lax.broadcasted_iota(jnp.int32, (8, 128), 1)
    stat_ref[...] = jnp.where(lane == 0, focal, jnp.where(lane == 1, count, 0.0))


def split3(x):
    hi = lax.reduce_precision(x, 8, 7)
    mid = lax.reduce_precision(x - hi, 8, 7)
    return [hi, mid, x - hi - mid]


def per_device(
    inputs, reduce_weight, spatial_weight, expand_weight, class_weight, anchor_labels, anchor_mask
):
    one = jnp.ones((1, ROWS, COLS), BF)
    none = jnp.zeros((CHANNELS - C - 2 * A - 1, ROWS, COLS), BF)
    fields = jnp.concatenate(
        [inputs[0], anchor_labels[0].astype(BF), anchor_mask[0].astype(BF), one, none], axis=0
    )
    fields = jnp.transpose(fields, (1, 0, 2))
    ahead = [(i, i + 1) for i in range(3)]
    back = [(i + 1, i) for i in range(3)]
    top = lax.ppermute(fields[ROWS - HALO :], "row", ahead)
    bottom = lax.ppermute(fields[:HALO], "row", back)
    pack = jax.ShapeDtypeStruct((CHANNELS, 256), BF)
    left_edge, right_edge = pl.pallas_call(
        pack_kernel,
        out_shape=(pack, pack),
        compiler_params=pltpu.CompilerParams(vmem_limit_bytes=56 << 20),
    )(fields, top, bottom)
    left = lax.ppermute(right_edge, "col", ahead)
    right = lax.ppermute(left_edge, "col", back)

    w2 = jnp.transpose(spatial_weight, (2, 0, 1, 3)).reshape(MID, 9 * MID)
    w2t = jnp.transpose(spatial_weight, (3, 0, 1, 2)).reshape(MID, 9 * MID)
    w3 = jnp.transpose(class_weight, (2, 0, 1, 3)).reshape(OUT, 9 * C)
    w3 = jnp.pad(w3, ((0, 136 - OUT), (0, 0)))
    w9 = class_weight.reshape(9, OUT, C)
    w3t = jnp.concatenate(
        [
            w9[:, :128].reshape(9 * 128, C),
            jnp.pad(w9[:, 128:], ((0, 0), (0, TAIL - 7), (0, 0))).reshape(9 * TAIL, C),
            jnp.zeros((8, C), BF),
        ],
        axis=0,
    ).T
    spread = np.zeros((136, CHANNELS - C), np.float32)
    for o in range(OUT):
        spread[o, o // K] = 1.0
        spread[o, A + o // K] = 16.0
    spread = jnp.asarray(spread, BF)

    shape = jax.ShapeDtypeStruct
    gclass, gred, gspat, gexp, stat = pl.pallas_call(
        main_kernel,
        out_shape=(
            shape((STACK, C), F32),
            shape((MID, C), F32),
            shape((9 * MID, MID), F32),
            shape((C, MID), F32),
            shape((8, 128), F32),
        ),
        scratch_shapes=[
            pltpu.VMEM((CHANNELS, WIDTH), BF),
            pltpu.VMEM((MID, WIDTH), BF),
            pltpu.VMEM((MID, WIDTH), BF),
            pltpu.VMEM((C, WIDTH), BF),
            pltpu.VMEM((128, WIDTH), BF),
            pltpu.VMEM((TAIL, WIDTH), F32),
            pltpu.VMEM((MID, WIDTH), BF),
            pltpu.VMEM((8, CHUNK), F32),
            pltpu.VMEM((8, CHUNK), F32),
        ],
        compiler_params=pltpu.CompilerParams(vmem_limit_bytes=56 << 20),
    )(
        fields, top, bottom, left, right,
        reduce_weight, w2, w2t, expand_weight, expand_weight.T, w3, w3t, spread,
    )

    focal, count = (stat[0, 0], stat[0, 1])
    flat = jnp.concatenate([gclass.reshape(-1), gred.reshape(-1), gspat.reshape(-1), gexp.reshape(-1)])
    size = flat.size
    share = -(-size // (128 * 128))
    flat = jnp.pad(flat, (0, share * 128 * 128 - size)).reshape(128, share, 128)
    stats = jnp.stack(split3(focal) + split3(count))
    stats = jnp.broadcast_to(jnp.pad(stats, (0, 122))[None, None], (128, 1, 128))
    sent = jnp.concatenate([flat, stats], axis=1).astype(BF)
    came = lax.all_to_all(sent, ALL, 0, 0, tiled=True)
    summed = jnp.sum(came.astype(F32), axis=0)
    focal = jnp.sum(summed[share, 0:3])
    count = jnp.sum(summed[share, 3:6])
    mine = (summed[:share] / count).astype(BF)
    copies = jnp.broadcast_to(mine[None], (128, share, 128))
    flat = lax.all_to_all(copies, ALL, 0, 0, tiled=True).astype(F32).reshape(-1)
    at = STACK * C
    rows = flat[:at].reshape(STACK, C)
    gclass = jnp.concatenate(
        [rows[: 9 * 128].reshape(9, 128, C), rows[9 * 128 : 9 * 136].reshape(9, TAIL, C)[:, :7]], axis=1
    ).reshape(3, 3, OUT, C)
    gred = flat[at : at + MID * C].reshape(MID, C)
    at = at + MID * C
    gspat = flat[at : at + 9 * MID * MID].reshape(3, 3, MID, MID)
    at = at + 9 * MID * MID
    gexp = flat[at : at + C * MID].reshape(C, MID)
    return (focal / count, gred, gspat, gexp, gclass)


def solution(mesh):
    maps = P("dp", None, "row", "col")
    return jax.shard_map(
        per_device,
        mesh=mesh,
        in_specs=(maps, P(), P(), P(), P(), maps, maps),
        out_specs=(P(), P(), P(), P(), P()),
        check_vma=False,
    )
```

```python
import jax
import jax.numpy as jnp
import numpy as np
from jax import lax
from jax.experimental import pallas as pl
from jax.experimental.pallas import tpu as pltpu
from jax.sharding import PartitionSpec as P

A = 9
K = 15
OUT = A * K
C = 256
MID = 64
HALO = 4
ROWS = 32
COLS = 128
FULL = ROWS + 2 * HALO
STRIDE = COLS + 2 * HALO
CHANNELS = 288
MARGIN = 256
WIDTH = 6400
CHUNK = 512
LABEL0 = C
MASK0 = C + A
ONE0 = C + 2 * A
TAGS = CHANNELS - C
TAIL = 8
STACK = 9 * 128 + 9 * TAIL + 8
ALL = ("dp", "row", "col")
DEVICES = 128
SHARE = 24
RED0 = 2 * STACK
SPAT0 = RED0 + 2 * MID
EXP0 = SPAT0 + 9 * MID // 2
STAT0 = EXP0 + C // 2
TAPS = [(dy - 1) * STRIDE + (dx - 1) for dy in range(3) for dx in range(3)]
BF = jnp.bfloat16
F32 = jnp.float32


def put(ref, rows, tile, value, lo, hi):
    lane = lax.broadcasted_iota(jnp.int32, value.shape, 1)
    where = slice(tile * 128, tile * 128 + 128)
    ref[rows, where] = jnp.where((lane >= lo) & (lane < hi), value, ref[rows, where])


BODY = slice(0, C)
REST = slice(C, CHANNELS)
BOTH = slice(0, CHANNELS)


def edges_kernel(maps_ref, tags_ref, left_ref, right_ref):
    left_ref[...] = jnp.zeros_like(left_ref)
    right_ref[...] = jnp.zeros_like(right_ref)
    for r in range(ROWS):
        at = HALO * r
        for rows, source in ((BODY, maps_ref[r]), (REST, tags_ref[r])):
            put(left_ref, rows, 0, pltpu.roll(source, at, 1), at, at + HALO)
            put(right_ref, rows, 0, pltpu.roll(source, (at + HALO) % 128, 1), at, at + HALO)


def corners_kernel(left_ref, right_ref, top_ref, bottom_ref, wide_left_ref, wide_right_ref):
    for edge_ref, wide_ref in ((left_ref, wide_left_ref), (right_ref, wide_right_ref)):
        wide_ref[:, :128] = edge_ref[...]
        wide_ref[:, 128:] = jnp.zeros_like(edge_ref)
    for h in range(2 * HALO):
        source = top_ref[h] if h < HALO else bottom_ref[h - HALO]
        at = HALO * h
        put(wide_left_ref, BOTH, 1, pltpu.roll(source, at, 1), at, at + HALO)
        put(wide_right_ref, BOTH, 1, pltpu.roll(source, at + HALO, 1), at, at + HALO)


def window(ref, rows, lane, shift):
    base = (shift // 128) * 128
    turn = shift - base
    if turn == 0:
        return ref[rows, pl.ds(pl.multiple_of(lane + base, 128), CHUNK)]
    wide = ref[rows, pl.ds(pl.multiple_of(lane + base, 128), CHUNK + 128)]
    return pltpu.roll(wide, CHUNK + 128 - turn, 1)[:, :CHUNK]


def interior(lane, shift):
    p = lane - MARGIN + shift + lax.broadcasted_iota(jnp.int32, (1, CHUNK), 1)
    r = (p * 30841) >> 22
    c = p - r * STRIDE
    return (r >= HALO) & (r < HALO + ROWS) & (c >= HALO) & (c < HALO + COLS)


def dot(a, b):
    return jnp.dot(a, b, preferred_element_type=F32)


def dot_nt(a, b):
    return lax.dot_general(a, b, (((1,), (1,)), ((), ())), preferred_element_type=F32)


def chunks(start, count, body):
    def step(j, carry):
        body(pl.multiple_of(MARGIN + start + j * CHUNK, 128))
        return carry

    lax.fori_loop(0, count, step, 0)


def main_kernel(
    maps_ref, tags_ref, top_ref, bottom_ref, left_ref, right_ref,
    wr_ref, w2_ref, w2t_ref, we_ref, wet_ref, w3_ref, w3t_ref, e_ref,
    out_ref,
    x_ref, first_ref, second_ref, block_ref, d_ref, dt_ref, ds_ref, facc_ref, cacc_ref,
    gclass_ref, gred_ref, gspat_ref, gexp_ref,
):
    for ref in (x_ref, first_ref, second_ref, block_ref, d_ref, dt_ref, ds_ref):
        ref[...] = jnp.zeros_like(ref)
    for ref in (gclass_ref, gred_ref, gspat_ref, gexp_ref, facc_ref, cacc_ref):
        ref[...] = jnp.zeros_like(ref)
    for r in range(FULL):
        if r < HALO:
            sources = ((BOTH, top_ref[r]),)
        elif r < HALO + ROWS:
            sources = ((BODY, maps_ref[r - HALO]), (REST, tags_ref[r - HALO]))
        else:
            sources = ((BOTH, bottom_ref[r - HALO - ROWS]),)
        at = MARGIN + r * STRIDE + HALO
        turn, tile = (at % 128, at // 128)
        for rows, source in sources:
            turned = pltpu.roll(source, turn, 1)
            put(x_ref, rows, tile, turned, turn, 128)
            put(x_ref, rows, tile + 1, turned, 0, turn)
        if HALO <= r < HALO + ROWS:
            spot = HALO * (r - HALO)
        else:
            spot = 128 + HALO * (r if r < HALO else r - ROWS)
        source = slice(spot // 128 * 128, spot // 128 * 128 + 128)
        for edge_ref, at in ((left_ref, MARGIN + r * STRIDE), (right_ref, MARGIN + r * STRIDE + HALO + COLS)):
            turned = pltpu.roll(edge_ref[:, source], (at - spot) % 128, 1)
            put(x_ref, BOTH, at // 128, turned, at % 128, at % 128 + HALO)

    def first_step(lane):
        x = x_ref[:C, pl.ds(lane, CHUNK)]
        first_ref[:, pl.ds(lane, CHUNK)] = jnp.maximum(dot(wr_ref[...], x), 0.0).astype(BF)

    chunks(0, 11, first_step)

    def block_step(lane):
        here = pl.ds(lane, CHUNK)
        stack = jnp.concatenate([window(first_ref, slice(None), lane, s) for s in TAPS], axis=0)
        second = jnp.maximum(dot(w2_ref[...], stack), 0.0)
        inside = x_ref[ONE0 - 2 : ONE0 + 14, here].astype(F32)[2:3]
        second = jnp.where(inside > 0.5, second, 0.0).astype(BF)
        second_ref[:, here] = second
        total = x_ref[:C, here].astype(F32) + dot(we_ref[...], second)
        block_ref[:, here] = jnp.maximum(total, 0.0).astype(BF)

    chunks(128, 11, block_step)

    channel = lax.broadcasted_iota(jnp.int32, (136, 1), 0)
    wanted = (channel - 15 * ((channel * 4370) >> 16) + 17).astype(F32)

    def logit_step(lane):
        here = pl.ds(lane, CHUNK)
        stack = jnp.concatenate([window(block_ref, slice(None), lane, s) for s in TAPS], axis=0)
        z = dot(w3_ref[...], stack)
        tags = x_ref[C:CHANNELS, here]
        code = dot(e_ref[...], tags)
        target = code == wanted
        counted = code > 15.5
        u = jnp.where(target, z, -z)
        alpha = jnp.where(target, 0.25, 0.75)
        e = jnp.exp(-jnp.abs(u))
        d = 1.0 / (1.0 + e)
        ed = e * d
        positive = u >= 0
        p = jnp.where(positive, ed, d)
        q = jnp.where(positive, d, ed)
        ls = jnp.minimum(u, 0.0) - jnp.log1p(e)
        ap2 = jnp.where(counted, alpha, 0.0) * p * p
        grad = ap2 * (2.0 * q * ls - p)
        grad = jnp.where(target, grad, -grad)
        d_ref[:, here] = grad[:128].astype(BF)
        dt_ref[:, here] = grad[128:].astype(BF).astype(F32)
        inner = interior(lane, 0)
        focal = jnp.where(inner, ap2 * ls, 0.0)
        facc_ref[...] -= jnp.sum(focal.reshape(17, 8, CHUNK), axis=0)
        labels = tags[:16].astype(F32)
        tag = lax.broadcasted_iota(jnp.int32, (16, CHUNK), 0)
        positives = jnp.where((labels > 0.5) & (tag < A) & inner, 1.0, 0.0)
        cacc_ref[...] += positives[:8] + positives[8:]

    chunks(256, 10, logit_step)

    def class_step(lane):
        here = pl.ds(lane, CHUNK)
        mains = [window(d_ref, slice(None), lane, -s) for s in TAPS]
        tails = [window(dt_ref, slice(None), lane, -s) for s in TAPS]
        inner = [interior(lane, -s) for s in TAPS]
        spare = jnp.zeros((8, CHUNK), F32)
        block = block_ref[:, here]
        stack = jnp.concatenate(
            mains + [jnp.concatenate(tails + [spare], axis=0).astype(BF)], axis=0
        )
        dblock = dot(w3t_ref[...], stack)
        dsum = jnp.where(block.astype(F32) > 0, dblock, 0.0).astype(BF)
        second = second_ref[:, here]
        within = interior(lane, 0)
        second32 = second.astype(F32)
        gexp_ref[...] += dot_nt(dsum, jnp.where(within, second32, 0.0).astype(BF))
        ds_ref[:, here] = jnp.where(second32 > 0, dot(wet_ref[...], dsum), 0.0).astype(BF)
        own = jnp.concatenate(
            [m * jnp.where(i, 1.0, 0.0).astype(BF) for m, i in zip(mains, inner)]
            + [
                jnp.concatenate(
                    [jnp.where(i, t, 0.0) for t, i in zip(tails, inner)] + [spare], axis=0
                ).astype(BF)
            ],
            axis=0,
        )
        gclass_ref[...] += dot_nt(own, block)

    chunks(384, 10, class_step)

    def first_back(lane):
        here = pl.ds(lane, CHUNK)
        parts = [window(ds_ref, slice(None), lane, -s) for s in TAPS]
        inner = [interior(lane, -s) for s in TAPS]
        first = first_ref[:, here]
        own = jnp.concatenate(
            [m * jnp.where(i, 1.0, 0.0).astype(BF) for m, i in zip(parts, inner)], axis=0
        )
        gspat_ref[...] += dot_nt(own, first)
        dfirst = dot(w2t_ref[...], jnp.concatenate(parts, axis=0))
        keep = (first.astype(F32) > 0) & interior(lane, 0)
        dfirst = jnp.where(keep, dfirst, 0.0).astype(BF)
        gred_ref[...] += dot_nt(dfirst, x_ref[:C, here])

    chunks(384, 10, first_back)

    out_ref[:STACK] = gclass_ref[:, :128].astype(BF)
    out_ref[STACK:RED0] = gclass_ref[:, 128:].astype(BF)
    out_ref[RED0 : RED0 + MID] = gred_ref[:, :128].astype(BF)
    out_ref[RED0 + MID : SPAT0] = gred_ref[:, 128:].astype(BF)
    half = 9 * MID // 2
    out_ref[SPAT0:EXP0] = jnp.concatenate([gspat_ref[:half], gspat_ref[half:]], axis=1).astype(BF)
    half = C // 2
    out_ref[EXP0:STAT0] = jnp.concatenate([gexp_ref[:half], gexp_ref[half:]], axis=1).astype(BF)
    out_ref[STAT0:] = jnp.zeros((DEVICES * SHARE - STAT0, 128), BF)
    focal = jnp.sum(facc_ref[...], keepdims=True)
    count = jnp.sum(cacc_ref[...], keepdims=True)
    out_ref[STAT0 : STAT0 + 16] = stat_rows(focal, count, 16).astype(BF)


def rounded(x):
    return x.astype(BF).astype(F32)


def stat_rows(focal, count, rows):
    lane = lax.broadcasted_iota(jnp.int32, (rows, 128), 1)
    out = jnp.zeros((rows, 128), F32)
    for at, value in ((0, focal), (3, count)):
        value = jnp.broadcast_to(value, (rows, 128))
        for k in range(3):
            piece = rounded(value)
            out = jnp.where(lane == at + k, piece, out)
            value = value - piece
    return out


def stat_values(row):
    lane = lax.broadcasted_iota(jnp.int32, row.shape, 1)
    focal = jnp.sum(jnp.where(lane < 3, row, 0.0), axis=1, keepdims=True)
    count = jnp.sum(jnp.where((lane >= 3) & (lane < 6), row, 0.0), axis=1, keepdims=True)
    return focal, count


def sum_kernel(index_ref, came_ref, copies_ref):
    total = came_ref[0].astype(F32)
    for k in range(1, DEVICES):
        total = total + came_ref[k].astype(F32)
    row = STAT0 % SHARE
    at = lax.broadcasted_iota(jnp.int32, (SHARE, 128), 0)
    focal, count = stat_values(total[row : row + 1])
    stats = stat_rows(focal, count, SHARE)
    total = jnp.where((at == row) & (index_ref[0] == STAT0 // SHARE), stats, total)
    total = total.astype(BF)
    for k in range(DEVICES):
        copies_ref[k] = total


def final_kernel(flat_ref, loss_ref, gred_ref, gspat_ref, gexp_ref, gclass_ref):
    focal, count = stat_values(flat_ref[STAT0 : STAT0 + 16].astype(F32)[:1])
    scale = 1.0 / count
    loss_ref[...] = focal * scale

    def rows(lo, n):
        return flat_ref[lo : lo + n].astype(F32) * scale

    for half in range(2):
        lanes = slice(half * 128, half * 128 + 128)
        tails = rows(half * STACK + 9 * 128, STACK - 9 * 128)
        for t in range(9):
            gclass_ref[t, :128, lanes] = rows(half * STACK + t * 128, 128)
            gclass_ref[t, 128:, lanes] = tails[t * TAIL : t * TAIL + 7]
        gred_ref[:, lanes] = rows(RED0 + half * MID, MID)
    spat = rows(SPAT0, 9 * MID // 2)
    gspat_ref[: 9 * MID // 2] = spat[:, :MID]
    gspat_ref[9 * MID // 2 :] = spat[:, MID:]
    expand = rows(EXP0, C // 2)
    gexp_ref[: C // 2] = expand[:, :MID]
    gexp_ref[C // 2 :] = expand[:, MID:]


def per_device(
    inputs, reduce_weight, spatial_weight, expand_weight, class_weight, anchor_labels, anchor_mask
):
    one = jnp.ones((1, ROWS, COLS), BF)
    none = jnp.zeros((TAGS - 2 * A - 1, ROWS, COLS), BF)
    tags = jnp.concatenate(
        [anchor_labels[0].astype(BF), anchor_mask[0].astype(BF), one, none], axis=0
    )

    def edge_rows(at):
        fields = jnp.concatenate([inputs[0, :, at : at + HALO], tags[:, at : at + HALO]], axis=0)
        return jnp.transpose(fields, (1, 0, 2))

    ahead = [(i, i + 1) for i in range(3)]
    back = [(i + 1, i) for i in range(3)]
    top = lax.ppermute(edge_rows(ROWS - HALO), "row", ahead)
    bottom = lax.ppermute(edge_rows(0), "row", back)
    maps = jnp.transpose(inputs[0], (1, 0, 2))
    tags = jnp.transpose(tags, (1, 0, 2))
    params = pltpu.CompilerParams(vmem_limit_bytes=56 << 20)
    pack = jax.ShapeDtypeStruct((CHANNELS, 128), BF)
    left_edge, right_edge = pl.pallas_call(
        edges_kernel, out_shape=(pack, pack), compiler_params=params
    )(maps, tags)
    pack = jax.ShapeDtypeStruct((CHANNELS, 256), BF)
    left_edge, right_edge = pl.pallas_call(
        corners_kernel, out_shape=(pack, pack), compiler_params=params
    )(left_edge, right_edge, top, bottom)
    left = lax.ppermute(right_edge, "col", ahead)
    right = lax.ppermute(left_edge, "col", back)

    w2 = jnp.transpose(spatial_weight, (2, 0, 1, 3)).reshape(MID, 9 * MID)
    w2t = jnp.transpose(spatial_weight, (3, 0, 1, 2)).reshape(MID, 9 * MID)
    w3 = jnp.transpose(class_weight, (2, 0, 1, 3)).reshape(OUT, 9 * C)
    w3 = jnp.pad(w3, ((0, 136 - OUT), (0, 0)))
    w9 = class_weight.reshape(9, OUT, C)
    w3t = jnp.concatenate(
        [
            w9[:, :128].reshape(9 * 128, C),
            jnp.pad(w9[:, 128:], ((0, 0), (0, TAIL - 7), (0, 0))).reshape(9 * TAIL, C),
            jnp.zeros((8, C), BF),
        ],
        axis=0,
    ).T
    spread = np.zeros((136, CHANNELS - C), np.float32)
    for o in range(OUT):
        spread[o, o // K] = 1.0
        spread[o, A + o // K] = 16.0
    spread = jnp.asarray(spread, BF)

    shape = jax.ShapeDtypeStruct
    out = pl.pallas_call(
        main_kernel,
        out_shape=shape((DEVICES * SHARE, 128), BF),
        scratch_shapes=[
            pltpu.VMEM((CHANNELS, WIDTH), BF),
            pltpu.VMEM((MID, WIDTH), BF),
            pltpu.VMEM((MID, WIDTH), BF),
            pltpu.VMEM((C, WIDTH), BF),
            pltpu.VMEM((128, WIDTH), BF),
            pltpu.VMEM((TAIL, WIDTH), F32),
            pltpu.VMEM((MID, WIDTH), BF),
            pltpu.VMEM((8, CHUNK), F32),
            pltpu.VMEM((8, CHUNK), F32),
            pltpu.VMEM((STACK, C), F32),
            pltpu.VMEM((MID, C), F32),
            pltpu.VMEM((9 * MID, MID), F32),
            pltpu.VMEM((C, MID), F32),
        ],
        compiler_params=params,
    )(
        maps, tags, top, bottom, left, right,
        reduce_weight, w2, w2t, expand_weight, expand_weight.T, w3, w3t, spread,
    )

    sent = out.reshape(DEVICES, SHARE, 128)
    came = lax.all_to_all(sent, ALL, 0, 0, tiled=True)
    index = lax.axis_index(ALL).astype(jnp.int32).reshape(1)
    copies = pl.pallas_call(
        sum_kernel,
        out_shape=shape((DEVICES, SHARE, 128), BF),
        in_specs=[
            pl.BlockSpec(memory_space=pltpu.SMEM),
            pl.BlockSpec(memory_space=pltpu.VMEM),
        ],
        compiler_params=params,
    )(index, came)
    flat = lax.all_to_all(copies, ALL, 0, 0, tiled=True).reshape(DEVICES * SHARE, 128)
    loss, gred, gspat, gexp, gclass = pl.pallas_call(
        final_kernel,
        out_shape=(
            shape((1, 1), F32),
            shape((MID, C), F32),
            shape((9 * MID, MID), F32),
            shape((C, MID), F32),
            shape((9, OUT, C), F32),
        ),
        compiler_params=params,
    )(flat)
    return (
        loss.reshape(()),
        gred,
        gspat.reshape(3, 3, MID, MID),
        gexp,
        gclass.reshape(3, 3, OUT, C),
    )


def solution(mesh):
    maps = P("dp", None, "row", "col")
    return jax.shard_map(
        per_device,
        mesh=mesh,
        in_specs=(maps, P(), P(), P(), P(), maps, maps),
        out_specs=(P(), P(), P(), P(), P()),
        check_vma=False,
    )
```

```python
import jax
import jax.numpy as jnp
import numpy as np
from jax import lax
from jax.experimental import pallas as pl
from jax.experimental.pallas import tpu as pltpu
from jax.sharding import PartitionSpec as P

A = 9
K = 15
OUT = A * K
C = 256
MID = 64
HALO = 4
ROWS = 32
COLS = 128
FULL = ROWS + 2 * HALO
STRIDE = COLS + 2 * HALO
CHANNELS = 288
MARGIN = 256
WIDTH = 6400
RIGHT = MARGIN + 5120
SPLIT = (
    (0, 2816, 2),
    (0, 2816, 2),
    (128, 2688, 2),
    (0, 2816, 2),
    (256, 1024, 5),
    (384, 2432, 2),
    (384, 2432, 2),
    (512, 2304, 2),
)
LABEL0 = C
MASK0 = C + A
ONE0 = C + 2 * A
TAGS = CHANNELS - C
TAIL = 8
STACK = 9 * 128 + 9 * TAIL + 8
ALL = ("dp", "row", "col")
DEVICES = 128
SHARE = 24
RED0 = 2 * STACK
SPAT0 = RED0 + 2 * MID
EXP0 = SPAT0 + 9 * MID // 2
STAT0 = EXP0 + C // 2
TAPS = [(dy - 1) * STRIDE + (dx - 1) for dy in range(3) for dx in range(3)]
BF = jnp.bfloat16
F32 = jnp.float32


def put(ref, rows, tile, value, lo, hi):
    lane = lax.broadcasted_iota(jnp.int32, value.shape, 1)
    where = slice(tile * 128, tile * 128 + 128)
    ref[rows, where] = jnp.where((lane >= lo) & (lane < hi), value, ref[rows, where])


BODY = slice(0, C)
REST = slice(C, CHANNELS)
BOTH = slice(0, CHANNELS)


def edges_kernel(maps_ref, tags_ref, left_ref, right_ref):
    left_ref[...] = jnp.zeros_like(left_ref)
    right_ref[...] = jnp.zeros_like(right_ref)
    for r in range(ROWS):
        at = HALO * r
        for rows, source in ((BODY, maps_ref[r]), (REST, tags_ref[r])):
            put(left_ref, rows, 0, pltpu.roll(source, at, 1), at, at + HALO)
            put(right_ref, rows, 0, pltpu.roll(source, (at + HALO) % 128, 1), at, at + HALO)


def corners_kernel(left_ref, right_ref, top_ref, bottom_ref, wide_left_ref, wide_right_ref):
    for edge_ref, wide_ref in ((left_ref, wide_left_ref), (right_ref, wide_right_ref)):
        wide_ref[:, :128] = edge_ref[...]
        wide_ref[:, 128:] = jnp.zeros_like(edge_ref)
    for h in range(2 * HALO):
        source = top_ref[h] if h < HALO else bottom_ref[h - HALO]
        at = HALO * h
        put(wide_left_ref, BOTH, 1, pltpu.roll(source, at, 1), at, at + HALO)
        put(wide_right_ref, BOTH, 1, pltpu.roll(source, at + HALO, 1), at, at + HALO)


def window(ref, rows, lane, shift, n):
    base = (shift // 128) * 128
    turn = shift - base
    if turn == 0:
        return ref[rows, pl.ds(pl.multiple_of(lane + base, 128), n)]
    wide = ref[rows, pl.ds(pl.multiple_of(lane + base, 128), n + 128)]
    return pltpu.roll(wide, n + 128 - turn, 1)[:, :n]


def interior(lane, shift, n):
    p = lane - MARGIN + shift + lax.broadcasted_iota(jnp.int32, (1, n), 1)
    r = (p * 30841) >> 22
    c = p - r * STRIDE
    return (r >= HALO) & (r < HALO + ROWS) & (c >= HALO) & (c < HALO + COLS)


def masked(value, mask):
    return value * jnp.where(mask, 1.0, 0.0).astype(BF)


def dot(a, b):
    return jnp.dot(a, b, preferred_element_type=F32)


def dot_nt(a, b):
    return lax.dot_general(a, b, (((1,), (1,)), ((), ())), preferred_element_type=F32)


def chunks(start, n, count, body):
    def step(j, carry):
        body(pl.multiple_of(MARGIN + start + j * n, 128), n)
        return carry

    lax.fori_loop(0, count, step, 0)


def across(ref, lane, sign, n):
    return jnp.concatenate([window(ref, slice(None), lane, sign * k, n) for k in (-1, 0, 1)], axis=0)


def down(ref, lane, sign, size, n):
    parts = [
        window(ref, slice(k * size, k * size + size), lane, sign * (k - 1) * STRIDE, n)
        for k in range(3)
    ]
    return parts[0] + parts[1] + parts[2]


def main_kernel(
    maps_ref, tags_ref, top_ref, bottom_ref, left_ref, right_ref,
    wr_ref, w2_ref, w2t_ref, we_ref, wet_ref, w3_ref, w3t_ref, e_ref,
    out_ref,
    x_ref, first_ref, second_ref, block_ref, d_ref, dt_ref, ds_ref, p_ref, facc_ref, cacc_ref,
    gclass_ref, gred_ref, gspat_ref, gexp_ref,
):
    for ref in (x_ref, first_ref, second_ref, block_ref, d_ref, dt_ref, ds_ref, p_ref):
        ref[:, : 2 * MARGIN] = jnp.zeros((ref.shape[0], 2 * MARGIN), ref.dtype)
        ref[:, RIGHT:] = jnp.zeros((ref.shape[0], WIDTH - RIGHT), ref.dtype)
    for ref in (gclass_ref, gred_ref, gspat_ref, gexp_ref, facc_ref, cacc_ref):
        ref[...] = jnp.zeros_like(ref)
    for r in range(FULL):
        if r < HALO:
            sources = ((BOTH, top_ref[r]),)
        elif r < HALO + ROWS:
            sources = ((BODY, maps_ref[r - HALO]), (REST, tags_ref[r - HALO]))
        else:
            sources = ((BOTH, bottom_ref[r - HALO - ROWS]),)
        at = MARGIN + r * STRIDE + HALO
        turn, tile = (at % 128, at // 128)
        for rows, source in sources:
            turned = pltpu.roll(source, turn, 1)
            put(x_ref, rows, tile, turned, turn, 128)
            put(x_ref, rows, tile + 1, turned, 0, turn)
        if HALO <= r < HALO + ROWS:
            spot = HALO * (r - HALO)
        else:
            spot = 128 + HALO * (r if r < HALO else r - ROWS)
        source = slice(spot // 128 * 128, spot // 128 * 128 + 128)
        for edge_ref, at in ((left_ref, MARGIN + r * STRIDE), (right_ref, MARGIN + r * STRIDE + HALO + COLS)):
            turned = pltpu.roll(edge_ref[:, source], (at - spot) % 128, 1)
            put(x_ref, BOTH, at // 128, turned, at % 128, at % 128 + HALO)

    def first_step(lane, n):
        x = x_ref[:C, pl.ds(lane, n)]
        first_ref[:, pl.ds(lane, n)] = jnp.maximum(dot(wr_ref[...], x), 0.0).astype(BF)

    chunks(*SPLIT[0], first_step)

    def spatial_step(lane, n):
        p_ref[: 3 * MID, pl.ds(lane, n)] = dot(w2_ref[...], across(first_ref, lane, 1, n))

    chunks(*SPLIT[1], spatial_step)

    def block_step(lane, n):
        here = pl.ds(lane, n)
        second = jnp.maximum(down(p_ref, lane, 1, MID, n), 0.0)
        inside = x_ref[ONE0 - 2 : ONE0 + 14, here].astype(F32)[2:3]
        second = jnp.where(inside > 0.5, second, 0.0).astype(BF)
        second_ref[:, here] = second
        total = x_ref[:C, here].astype(F32) + dot(we_ref[...], second)
        block_ref[:, here] = jnp.maximum(total, 0.0).astype(BF)

    chunks(*SPLIT[2], block_step)

    def class_step(lane, n):
        p_ref[:, pl.ds(lane, n)] = dot(w3_ref[...], across(block_ref, lane, 1, n))

    chunks(*SPLIT[3], class_step)

    channel = lax.broadcasted_iota(jnp.int32, (136, 1), 0)
    wanted = (channel - 15 * ((channel * 4370) >> 16) + 17).astype(F32)

    def focal_step(lane, n):
        here = pl.ds(lane, n)
        z = down(p_ref, lane, 1, 136, n)
        tags = x_ref[C:CHANNELS, here]
        code = dot(e_ref[...], tags)
        target = code == wanted
        counted = code > 15.5
        u = jnp.where(target, z, -z)
        alpha = jnp.where(target, 0.25, 0.75)
        e = jnp.exp(-jnp.abs(u))
        d = 1.0 / (1.0 + e)
        ed = e * d
        positive = u >= 0
        p = jnp.where(positive, ed, d)
        q = jnp.where(positive, d, ed)
        ls = jnp.minimum(u, 0.0) - jnp.log1p(e)
        ap2 = jnp.where(counted, alpha, 0.0) * p * p
        grad = ap2 * (2.0 * q * ls - p)
        grad = jnp.where(target, grad, -grad)
        d_ref[:, here] = grad[:128].astype(BF)
        dt_ref[:, here] = grad[128:].astype(BF).astype(F32)
        inner = interior(lane, 0, n)
        focal = jnp.where(inner, ap2 * ls, 0.0)
        facc_ref[...] -= jnp.sum(focal.reshape(17, 8, n), axis=0)
        labels = tags[:16].astype(F32)
        tag = lax.broadcasted_iota(jnp.int32, (16, n), 0)
        positives = jnp.where((labels > 0.5) & (tag < A) & inner, 1.0, 0.0)
        cacc_ref[...] += positives[:8] + positives[8:]

    chunks(*SPLIT[4], focal_step)

    def class_back(lane, n):
        here = pl.ds(lane, n)
        mains = [window(d_ref, slice(None), lane, -s, n) for s in TAPS]
        tails = [window(dt_ref, slice(None), lane, -s, n) for s in TAPS]
        inner = [interior(lane, -s, n) for s in TAPS]
        spare = jnp.zeros((8, n), F32)
        block = block_ref[:, here]
        stack = jnp.concatenate(
            mains + [jnp.concatenate(tails + [spare], axis=0).astype(BF)], axis=0
        )
        dblock = dot(w3t_ref[...], stack)
        dsum = jnp.where(block.astype(F32) > 0, dblock, 0.0).astype(BF)
        second = second_ref[:, here]
        within = interior(lane, 0, n)
        gexp_ref[...] += dot_nt(masked(second, within), dsum)
        dsecond = jnp.where(second.astype(F32) > 0, dot(wet_ref[...], dsum), 0.0)
        ds_ref[:, here] = dsecond.astype(BF)
        own = jnp.concatenate(
            [masked(m, i) for m, i in zip(mains, inner)]
            + [
                jnp.concatenate(
                    [jnp.where(i, t, 0.0) for t, i in zip(tails, inner)] + [spare], axis=0
                ).astype(BF)
            ],
            axis=0,
        )
        gclass_ref[...] += dot_nt(own, block)

    chunks(*SPLIT[5], class_back)

    def spatial_back(lane, n):
        stack = across(ds_ref, lane, -1, n)
        p_ref[: 3 * MID, pl.ds(lane, n)] = dot(w2t_ref[...], stack)
        own = jnp.concatenate(
            [
                masked(stack[k * MID : k * MID + MID], interior(lane, 1 - k, n))
                for k in range(3)
            ],
            axis=0,
        )
        first = jnp.concatenate(
            [window(first_ref, slice(None), lane, k * STRIDE, n) for k in (-1, 0, 1)], axis=0
        )
        gspat_ref[...] += dot_nt(own, first)

    chunks(*SPLIT[6], spatial_back)

    def first_back(lane, n):
        here = pl.ds(lane, n)
        dfirst = down(p_ref, lane, -1, MID, n)
        keep = (first_ref[:, here].astype(F32) > 0) & interior(lane, 0, n)
        dfirst = jnp.where(keep, dfirst, 0.0).astype(BF)
        gred_ref[...] += dot_nt(dfirst, x_ref[:C, here])

    chunks(*SPLIT[7], first_back)

    out_ref[:STACK] = gclass_ref[:, :128].astype(BF)
    out_ref[STACK:RED0] = gclass_ref[:, 128:].astype(BF)
    out_ref[RED0 : RED0 + MID] = gred_ref[:, :128].astype(BF)
    out_ref[RED0 + MID : SPAT0] = gred_ref[:, 128:].astype(BF)
    out_ref[SPAT0 : SPAT0 + 3 * MID] = gspat_ref[:, : 2 * MID].astype(BF)
    half = 3 * MID // 2
    out_ref[SPAT0 + 3 * MID : EXP0] = jnp.concatenate(
        [gspat_ref[:half, 2 * MID :], gspat_ref[half:, 2 * MID :]], axis=1
    ).astype(BF)
    out_ref[EXP0 : EXP0 + MID] = gexp_ref[:, :128].astype(BF)
    out_ref[EXP0 + MID : STAT0] = gexp_ref[:, 128:].astype(BF)
    out_ref[STAT0:] = jnp.zeros((DEVICES * SHARE - STAT0, 128), BF)
    focal = jnp.sum(facc_ref[...], keepdims=True)
    count = jnp.sum(cacc_ref[...], keepdims=True)
    out_ref[STAT0 : STAT0 + 16] = stat_rows(focal, count, 16).astype(BF)


def rounded(x):
    return x.astype(BF).astype(F32)


def stat_rows(focal, count, rows):
    lane = lax.broadcasted_iota(jnp.int32, (rows, 128), 1)
    out = jnp.zeros((rows, 128), F32)
    for at, value in ((0, focal), (3, count)):
        value = jnp.broadcast_to(value, (rows, 128))
        for k in range(3):
            piece = rounded(value)
            out = jnp.where(lane == at + k, piece, out)
            value = value - piece
    return out


def stat_values(row):
    lane = lax.broadcasted_iota(jnp.int32, row.shape, 1)
    focal = jnp.sum(jnp.where(lane < 3, row, 0.0), axis=1, keepdims=True)
    count = jnp.sum(jnp.where((lane >= 3) & (lane < 6), row, 0.0), axis=1, keepdims=True)
    return focal, count


def sum_kernel(index_ref, came_ref, copies_ref):
    total = came_ref[0].astype(F32)
    for k in range(1, DEVICES):
        total = total + came_ref[k].astype(F32)
    row = STAT0 % SHARE
    at = lax.broadcasted_iota(jnp.int32, (SHARE, 128), 0)
    focal, count = stat_values(total[row : row + 1])
    stats = stat_rows(focal, count, SHARE)
    total = jnp.where((at == row) & (index_ref[0] == STAT0 // SHARE), stats, total)
    total = total.astype(BF)
    for k in range(DEVICES):
        copies_ref[k] = total


def final_kernel(flat_ref, loss_ref, gred_ref, gspat_ref, gexp_ref, gclass_ref):
    focal, count = stat_values(flat_ref[STAT0 : STAT0 + 16].astype(F32)[:1])
    scale = 1.0 / count
    loss_ref[...] = focal * scale

    def rows(lo, n):
        return flat_ref[lo : lo + n].astype(F32) * scale

    for half in range(2):
        lanes = slice(half * 128, half * 128 + 128)
        tails = rows(half * STACK + 9 * 128, STACK - 9 * 128)
        for t in range(9):
            gclass_ref[t, :128, lanes] = rows(half * STACK + t * 128, 128)
            gclass_ref[t, 128:, lanes] = tails[t * TAIL : t * TAIL + 7]
        gred_ref[:, lanes] = rows(RED0 + half * MID, MID)
        gexp_ref[:, lanes] = rows(EXP0 + half * MID, MID)
    spat = rows(SPAT0, 3 * MID)
    last = rows(SPAT0 + 3 * MID, 3 * MID // 2)
    half = 3 * MID // 2
    for dx in range(3):
        for dy in range(2):
            gspat_ref[3 * dy + dx] = spat[dx * MID : dx * MID + MID, dy * MID : dy * MID + MID]
    gspat_ref[6] = last[:MID, :MID]
    gspat_ref[7, : half - MID] = last[MID:, :MID]
    gspat_ref[7, half - MID :] = last[: 2 * MID - half, MID:]
    gspat_ref[8] = last[2 * MID - half :, MID:]


def per_device(
    inputs, reduce_weight, spatial_weight, expand_weight, class_weight, anchor_labels, anchor_mask
):
    one = jnp.ones((1, ROWS, COLS), BF)
    none = jnp.zeros((TAGS - 2 * A - 1, ROWS, COLS), BF)
    tags = jnp.concatenate(
        [anchor_labels[0].astype(BF), anchor_mask[0].astype(BF), one, none], axis=0
    )

    def edge_rows(at):
        fields = jnp.concatenate([inputs[0, :, at : at + HALO], tags[:, at : at + HALO]], axis=0)
        return jnp.transpose(fields, (1, 0, 2))

    ahead = [(i, i + 1) for i in range(3)]
    back = [(i + 1, i) for i in range(3)]
    top = lax.ppermute(edge_rows(ROWS - HALO), "row", ahead)
    bottom = lax.ppermute(edge_rows(0), "row", back)
    maps = jnp.transpose(inputs[0], (1, 0, 2))
    tags = jnp.transpose(tags, (1, 0, 2))
    params = pltpu.CompilerParams(vmem_limit_bytes=56 << 20)
    pack = jax.ShapeDtypeStruct((CHANNELS, 128), BF)
    left_edge, right_edge = pl.pallas_call(
        edges_kernel, out_shape=(pack, pack), compiler_params=params
    )(maps, tags)
    pack = jax.ShapeDtypeStruct((CHANNELS, 256), BF)
    left_edge, right_edge = pl.pallas_call(
        corners_kernel, out_shape=(pack, pack), compiler_params=params
    )(left_edge, right_edge, top, bottom)
    left = lax.ppermute(right_edge, "col", ahead)
    right = lax.ppermute(left_edge, "col", back)

    w2 = jnp.transpose(spatial_weight, (0, 2, 1, 3)).reshape(3 * MID, 3 * MID)
    w2t = jnp.transpose(spatial_weight, (0, 3, 1, 2)).reshape(3 * MID, 3 * MID)
    w3 = jnp.pad(class_weight, ((0, 0), (0, 0), (0, 136 - OUT), (0, 0)))
    w3 = jnp.transpose(w3, (0, 2, 1, 3)).reshape(3 * 136, 3 * C)
    w9 = class_weight.reshape(9, OUT, C)
    w3t = jnp.concatenate(
        [
            w9[:, :128].reshape(9 * 128, C),
            jnp.pad(w9[:, 128:], ((0, 0), (0, TAIL - 7), (0, 0))).reshape(9 * TAIL, C),
            jnp.zeros((8, C), BF),
        ],
        axis=0,
    ).T
    spread = np.zeros((136, CHANNELS - C), np.float32)
    for o in range(OUT):
        spread[o, o // K] = 1.0
        spread[o, A + o // K] = 16.0
    spread = jnp.asarray(spread, BF)

    shape = jax.ShapeDtypeStruct
    out = pl.pallas_call(
        main_kernel,
        out_shape=shape((DEVICES * SHARE, 128), BF),
        scratch_shapes=[
            pltpu.VMEM((CHANNELS, WIDTH), BF),
            pltpu.VMEM((MID, WIDTH), BF),
            pltpu.VMEM((MID, WIDTH), BF),
            pltpu.VMEM((C, WIDTH), BF),
            pltpu.VMEM((128, WIDTH), BF),
            pltpu.VMEM((TAIL, WIDTH), F32),
            pltpu.VMEM((MID, WIDTH), BF),
            pltpu.VMEM((3 * 136, WIDTH), F32),
            pltpu.VMEM((8, SPLIT[4][1]), F32),
            pltpu.VMEM((8, SPLIT[4][1]), F32),
            pltpu.VMEM((STACK, C), F32),
            pltpu.VMEM((MID, C), F32),
            pltpu.VMEM((3 * MID, 3 * MID), F32),
            pltpu.VMEM((MID, C), F32),
        ],
        compiler_params=params,
    )(
        maps, tags, top, bottom, left, right,
        reduce_weight, w2, w2t, expand_weight, expand_weight.T, w3, w3t, spread,
    )

    sent = out.reshape(DEVICES, SHARE, 128)
    came = lax.all_to_all(sent, ALL, 0, 0, tiled=True)
    index = lax.axis_index(ALL).astype(jnp.int32).reshape(1)
    copies = pl.pallas_call(
        sum_kernel,
        out_shape=shape((DEVICES, SHARE, 128), BF),
        in_specs=[
            pl.BlockSpec(memory_space=pltpu.SMEM),
            pl.BlockSpec(memory_space=pltpu.VMEM),
        ],
        compiler_params=params,
    )(index, came)
    flat = lax.all_to_all(copies, ALL, 0, 0, tiled=True).reshape(DEVICES * SHARE, 128)
    loss, gred, gspat, gexp, gclass = pl.pallas_call(
        final_kernel,
        out_shape=(
            shape((1, 1), F32),
            shape((MID, C), F32),
            shape((9, MID, MID), F32),
            shape((MID, C), F32),
            shape((9, OUT, C), F32),
        ),
        compiler_params=params,
    )(flat)
    return (
        loss.reshape(()),
        gred,
        gspat.reshape(3, 3, MID, MID),
        gexp.T,
        gclass.reshape(3, 3, OUT, C),
    )


def solution(mesh):
    maps = P("dp", None, "row", "col")
    return jax.shard_map(
        per_device,
        mesh=mesh,
        in_specs=(maps, P(), P(), P(), P(), maps, maps),
        out_specs=(P(), P(), P(), P(), P()),
        check_vma=False,
    )
```

```python
import jax
import jax.numpy as jnp
import numpy as np
from jax import lax
from jax.experimental import pallas as pl
from jax.experimental.pallas import tpu as pltpu
from jax.sharding import PartitionSpec as P

A = 9
K = 15
OUT = A * K
C = 256
MID = 64
HALO = 4
ROWS = 32
COLS = 128
FULL = ROWS + 2 * HALO
STRIDE = COLS + 2 * HALO
CHANNELS = 288
MARGIN = 256
WIDTH = 6656
RIGHT = MARGIN + 5120
PIPE = 640
SPLIT = (
    (0, 2816, 2),
    (0, 2816, 2),
    (128, 2688, 2),
    (0, PIPE, 9),
    (256, PIPE, 8),
    (384, 2432, 2),
    (384, 2432, 2),
    (512, 2304, 2),
)
LABEL0 = C
MASK0 = C + A
ONE0 = C + 2 * A
TAGS = CHANNELS - C
TAIL = 8
STACK = 9 * 128 + 9 * TAIL + 8
ALL = ("dp", "row", "col")
DEVICES = 128
SHARE = 24
RED0 = 2 * STACK
SPAT0 = RED0 + 2 * MID
EXP0 = SPAT0 + 9 * MID // 2
STAT0 = EXP0 + C // 2
TAPS = [(dy - 1) * STRIDE + (dx - 1) for dy in range(3) for dx in range(3)]
BF = jnp.bfloat16
F32 = jnp.float32


def put(ref, rows, tile, value, lo, hi):
    lane = lax.broadcasted_iota(jnp.int32, value.shape, 1)
    where = slice(tile * 128, tile * 128 + 128)
    ref[rows, where] = jnp.where((lane >= lo) & (lane < hi), value, ref[rows, where])


BODY = slice(0, C)
REST = slice(C, CHANNELS)
BOTH = slice(0, CHANNELS)


def place(ref, rows, source, r):
    at = MARGIN + r * STRIDE + HALO
    turn, tile = (at % 128, at // 128)
    turned = pltpu.roll(source, turn, 1)
    put(ref, rows, tile, turned, turn, 128)
    put(ref, rows, tile + 1, turned, 0, turn)


def edges_kernel(maps_ref, tags_ref, left_ref, right_ref, x_ref):
    x_ref[...] = jnp.zeros_like(x_ref)
    left_ref[...] = jnp.zeros_like(left_ref)
    right_ref[...] = jnp.zeros_like(right_ref)
    for r in range(ROWS):
        at = HALO * r
        for rows, source in ((BODY, maps_ref[r]), (REST, tags_ref[r])):
            put(left_ref, rows, 0, pltpu.roll(source, at, 1), at, at + HALO)
            put(right_ref, rows, 0, pltpu.roll(source, (at + HALO) % 128, 1), at, at + HALO)
            place(x_ref, rows, source, r + HALO)


def corners_kernel(left_ref, right_ref, top_ref, bottom_ref, wide_left_ref, wide_right_ref):
    for edge_ref, wide_ref in ((left_ref, wide_left_ref), (right_ref, wide_right_ref)):
        wide_ref[:, :128] = edge_ref[...]
        wide_ref[:, 128:] = jnp.zeros_like(edge_ref)
    for h in range(2 * HALO):
        source = top_ref[h] if h < HALO else bottom_ref[h - HALO]
        at = HALO * h
        put(wide_left_ref, BOTH, 1, pltpu.roll(source, at, 1), at, at + HALO)
        put(wide_right_ref, BOTH, 1, pltpu.roll(source, at + HALO, 1), at, at + HALO)


def aligned(lane):
    return lane if isinstance(lane, int) else pl.multiple_of(lane, 128)


def window(ref, rows, lane, shift, n):
    base = (shift // 128) * 128
    turn = shift - base
    if turn == 0:
        return ref[rows, pl.ds(aligned(lane + base), n)]
    wide = ref[rows, pl.ds(aligned(lane + base), n + 128)]
    return pltpu.roll(wide, n + 128 - turn, 1)[:, :n]


def interior(lane, shift, n):
    p = lane - MARGIN + shift + lax.broadcasted_iota(jnp.int32, (1, n), 1)
    r = (p * 30841) >> 22
    c = p - r * STRIDE
    return (r >= HALO) & (r < HALO + ROWS) & (c >= HALO) & (c < HALO + COLS)


def masked(value, mask):
    return value * jnp.where(mask, 1.0, 0.0).astype(BF)


def dot(a, b):
    return jnp.dot(a, b, preferred_element_type=F32)


def dot_nt(a, b):
    return lax.dot_general(a, b, (((1,), (1,)), ((), ())), preferred_element_type=F32)


def chunks(start, n, count, body):
    def step(j, carry):
        body(pl.multiple_of(MARGIN + start + j * n, 128), n)
        return carry

    lax.fori_loop(0, count, step, 0)


def across(ref, lane, sign, n):
    return jnp.concatenate([window(ref, slice(None), lane, sign * k, n) for k in (-1, 0, 1)], axis=0)


def down(ref, lane, sign, size, n):
    parts = [
        window(ref, slice(k * size, k * size + size), lane, sign * (k - 1) * STRIDE, n)
        for k in range(3)
    ]
    return parts[0] + parts[1] + parts[2]


def main_kernel(
    x0_ref, top_ref, bottom_ref, left_ref, right_ref,
    wr_ref, w2_ref, w2t_ref, we_ref, wet_ref, w3_ref, w3t_ref, e_ref,
    out_ref,
    x_ref, first_ref, second_ref, block_ref, d_ref, dt_ref, ds_ref, p_ref, facc_ref, cacc_ref,
    gclass_ref, gred_ref, gspat_ref, gexp_ref, sem,
):
    copy = pltpu.make_async_copy(x0_ref, x_ref, sem)
    copy.start()
    for ref in (first_ref, second_ref, block_ref, d_ref, dt_ref, ds_ref, p_ref):
        ref[:, : 2 * MARGIN] = jnp.zeros((ref.shape[0], 2 * MARGIN), ref.dtype)
        ref[:, RIGHT:] = jnp.zeros((ref.shape[0], WIDTH - RIGHT), ref.dtype)
    for ref in (gclass_ref, gred_ref, gspat_ref, gexp_ref, facc_ref, cacc_ref):
        ref[...] = jnp.zeros_like(ref)
    copy.wait()
    for r in range(FULL):
        if r < HALO:
            place(x_ref, BOTH, top_ref[r], r)
        elif r >= HALO + ROWS:
            place(x_ref, BOTH, bottom_ref[r - HALO - ROWS], r)
        if HALO <= r < HALO + ROWS:
            spot = HALO * (r - HALO)
        else:
            spot = 128 + HALO * (r if r < HALO else r - ROWS)
        source = slice(spot // 128 * 128, spot // 128 * 128 + 128)
        for edge_ref, at in ((left_ref, MARGIN + r * STRIDE), (right_ref, MARGIN + r * STRIDE + HALO + COLS)):
            turned = pltpu.roll(edge_ref[:, source], (at - spot) % 128, 1)
            put(x_ref, BOTH, at // 128, turned, at % 128, at % 128 + HALO)

    def first_step(lane, n):
        x = x_ref[:C, pl.ds(lane, n)]
        first_ref[:, pl.ds(lane, n)] = jnp.maximum(dot(wr_ref[...], x), 0.0).astype(BF)

    chunks(*SPLIT[0], first_step)

    def spatial_step(lane, n):
        p_ref[: 3 * MID, pl.ds(lane, n)] = dot(w2_ref[...], across(first_ref, lane, 1, n))

    chunks(*SPLIT[1], spatial_step)

    def block_step(lane, n):
        here = pl.ds(lane, n)
        second = jnp.maximum(down(p_ref, lane, 1, MID, n), 0.0)
        inside = x_ref[ONE0 - 2 : ONE0 + 14, here].astype(F32)[2:3]
        second = jnp.where(inside > 0.5, second, 0.0).astype(BF)
        second_ref[:, here] = second
        total = x_ref[:C, here].astype(F32) + dot(we_ref[...], second)
        block_ref[:, here] = jnp.maximum(total, 0.0).astype(BF)

    chunks(*SPLIT[2], block_step)

    def class_step(lane, n):
        p_ref[:, pl.ds(lane, n)] = dot(w3_ref[...], across(block_ref, lane, 1, n))

    channel = lax.broadcasted_iota(jnp.int32, (136, 1), 0)
    wanted = (channel - 15 * ((channel * 4370) >> 16) + 17).astype(F32)

    def focal_step(lane, n):
        here = pl.ds(lane, n)
        z = down(p_ref, lane, 1, 136, n)
        tags = x_ref[C:CHANNELS, here]
        code = dot(e_ref[...], tags)
        target = code == wanted
        counted = code > 15.5
        u = jnp.where(target, z, -z)
        alpha = jnp.where(target, 0.25, 0.75)
        e = jnp.exp(-jnp.abs(u))
        d = 1.0 / (1.0 + e)
        ed = e * d
        positive = u >= 0
        p = jnp.where(positive, ed, d)
        q = jnp.where(positive, d, ed)
        ls = jnp.minimum(u, 0.0) - jnp.log1p(e)
        ap2 = jnp.where(counted, alpha, 0.0) * p * p
        grad = ap2 * (2.0 * q * ls - p)
        grad = jnp.where(target, grad, -grad)
        d_ref[:, here] = grad[:128].astype(BF)
        dt_ref[:, here] = grad[128:].astype(BF).astype(F32)
        inner = interior(lane, 0, n)
        focal = jnp.where(inner, ap2 * ls, 0.0)
        facc_ref[...] -= jnp.sum(focal.reshape(17, 8, n), axis=0)
        labels = tags[:16].astype(F32)
        tag = lax.broadcasted_iota(jnp.int32, (16, n), 0)
        positives = jnp.where((labels > 0.5) & (tag < A) & inner, 1.0, 0.0)
        cacc_ref[...] += positives[:8] + positives[8:]

    begin, n, count = SPLIT[3]
    for j in range(count + 2):
        if j >= 2 and j - 2 < SPLIT[4][2]:
            for k in range(0, n, 128):
                focal_step(MARGIN + SPLIT[4][0] + (j - 2) * n + k, 128)
        if j < count:
            class_step(MARGIN + begin + j * n, n)

    def class_back(lane, n):
        here = pl.ds(lane, n)
        mains = [window(d_ref, slice(None), lane, -s, n) for s in TAPS]
        tails = [window(dt_ref, slice(None), lane, -s, n) for s in TAPS]
        inner = [interior(lane, -s, n) for s in TAPS]
        spare = jnp.zeros((8, n), F32)
        block = block_ref[:, here]
        stack = jnp.concatenate(
            mains + [jnp.concatenate(tails + [spare], axis=0).astype(BF)], axis=0
        )
        dblock = dot(w3t_ref[...], stack)
        dsum = jnp.where(block.astype(F32) > 0, dblock, 0.0).astype(BF)
        second = second_ref[:, here]
        within = interior(lane, 0, n)
        gexp_ref[...] += dot_nt(masked(second, within), dsum)
        dsecond = jnp.where(second.astype(F32) > 0, dot(wet_ref[...], dsum), 0.0)
        ds_ref[:, here] = dsecond.astype(BF)
        own = jnp.concatenate(
            [masked(m, i) for m, i in zip(mains, inner)]
            + [
                jnp.concatenate(
                    [jnp.where(i, t, 0.0) for t, i in zip(tails, inner)] + [spare], axis=0
                ).astype(BF)
            ],
            axis=0,
        )
        gclass_ref[...] += dot_nt(own, block)

    chunks(*SPLIT[5], class_back)

    def spatial_back(lane, n):
        stack = across(ds_ref, lane, -1, n)
        p_ref[: 3 * MID, pl.ds(lane, n)] = dot(w2t_ref[...], stack)
        own = jnp.concatenate(
            [
                masked(stack[k * MID : k * MID + MID], interior(lane, 1 - k, n))
                for k in range(3)
            ],
            axis=0,
        )
        first = jnp.concatenate(
            [window(first_ref, slice(None), lane, k * STRIDE, n) for k in (-1, 0, 1)], axis=0
        )
        gspat_ref[...] += dot_nt(own, first)

    chunks(*SPLIT[6], spatial_back)

    def first_back(lane, n):
        here = pl.ds(lane, n)
        dfirst = down(p_ref, lane, -1, MID, n)
        keep = (first_ref[:, here].astype(F32) > 0) & interior(lane, 0, n)
        dfirst = jnp.where(keep, dfirst, 0.0).astype(BF)
        gred_ref[...] += dot_nt(dfirst, x_ref[:C, here])

    chunks(*SPLIT[7], first_back)

    out_ref[:STACK] = gclass_ref[:, :128].astype(BF)
    out_ref[STACK:RED0] = gclass_ref[:, 128:].astype(BF)
    out_ref[RED0 : RED0 + MID] = gred_ref[:, :128].astype(BF)
    out_ref[RED0 + MID : SPAT0] = gred_ref[:, 128:].astype(BF)
    out_ref[SPAT0 : SPAT0 + 3 * MID] = gspat_ref[:, : 2 * MID].astype(BF)
    half = 3 * MID // 2
    out_ref[SPAT0 + 3 * MID : EXP0] = jnp.concatenate(
        [gspat_ref[:half, 2 * MID :], gspat_ref[half:, 2 * MID :]], axis=1
    ).astype(BF)
    out_ref[EXP0 : EXP0 + MID] = gexp_ref[:, :128].astype(BF)
    out_ref[EXP0 + MID : STAT0] = gexp_ref[:, 128:].astype(BF)
    out_ref[STAT0:] = jnp.zeros((DEVICES * SHARE - STAT0, 128), BF)
    focal = jnp.sum(facc_ref[...], keepdims=True)
    count = jnp.sum(cacc_ref[...], keepdims=True)
    out_ref[STAT0 : STAT0 + 16] = stat_rows(focal, count, 16).astype(BF)


def rounded(x):
    return x.astype(BF).astype(F32)


def stat_rows(focal, count, rows):
    lane = lax.broadcasted_iota(jnp.int32, (rows, 128), 1)
    out = jnp.zeros((rows, 128), F32)
    for at, value in ((0, focal), (3, count)):
        value = jnp.broadcast_to(value, (rows, 128))
        for k in range(3):
            piece = rounded(value)
            out = jnp.where(lane == at + k, piece, out)
            value = value - piece
    return out


def stat_values(row):
    lane = lax.broadcasted_iota(jnp.int32, row.shape, 1)
    focal = jnp.sum(jnp.where(lane < 3, row, 0.0), axis=1, keepdims=True)
    count = jnp.sum(jnp.where((lane >= 3) & (lane < 6), row, 0.0), axis=1, keepdims=True)
    return focal, count


def sum_kernel(index_ref, came_ref, copies_ref):
    total = came_ref[0].astype(F32)
    for k in range(1, DEVICES):
        total = total + came_ref[k].astype(F32)
    row = STAT0 % SHARE
    at = lax.broadcasted_iota(jnp.int32, (SHARE, 128), 0)
    focal, count = stat_values(total[row : row + 1])
    stats = stat_rows(focal, count, SHARE)
    total = jnp.where((at == row) & (index_ref[0] == STAT0 // SHARE), stats, total)
    total = total.astype(BF)
    for k in range(DEVICES):
        copies_ref[k] = total


def final_kernel(flat_ref, loss_ref, gred_ref, gspat_ref, gexp_ref, gclass_ref):
    focal, count = stat_values(flat_ref[STAT0 : STAT0 + 16].astype(F32)[:1])
    scale = 1.0 / count
    loss_ref[...] = focal * scale

    def rows(lo, n):
        return flat_ref[lo : lo + n].astype(F32) * scale

    for half in range(2):
        lanes = slice(half * 128, half * 128 + 128)
        tails = rows(half * STACK + 9 * 128, STACK - 9 * 128)
        for t in range(9):
            gclass_ref[t, :128, lanes] = rows(half * STACK + t * 128, 128)
            gclass_ref[t, 128:, lanes] = tails[t * TAIL : t * TAIL + 7]
        gred_ref[:, lanes] = rows(RED0 + half * MID, MID)
        gexp_ref[:, lanes] = rows(EXP0 + half * MID, MID)
    spat = rows(SPAT0, 3 * MID)
    last = rows(SPAT0 + 3 * MID, 3 * MID // 2)
    half = 3 * MID // 2
    for dx in range(3):
        for dy in range(2):
            gspat_ref[3 * dy + dx] = spat[dx * MID : dx * MID + MID, dy * MID : dy * MID + MID]
    gspat_ref[6] = last[:MID, :MID]
    gspat_ref[7, : half - MID] = last[MID:, :MID]
    gspat_ref[7, half - MID :] = last[: 2 * MID - half, MID:]
    gspat_ref[8] = last[2 * MID - half :, MID:]


def per_device(
    inputs, reduce_weight, spatial_weight, expand_weight, class_weight, anchor_labels, anchor_mask
):
    one = jnp.ones((1, ROWS, COLS), BF)
    none = jnp.zeros((TAGS - 2 * A - 1, ROWS, COLS), BF)
    tags = jnp.concatenate(
        [anchor_labels[0].astype(BF), anchor_mask[0].astype(BF), one, none], axis=0
    )

    def edge_rows(at):
        fields = jnp.concatenate([inputs[0, :, at : at + HALO], tags[:, at : at + HALO]], axis=0)
        return jnp.transpose(fields, (1, 0, 2))

    ahead = [(i, i + 1) for i in range(3)]
    back = [(i + 1, i) for i in range(3)]
    top = lax.ppermute(edge_rows(ROWS - HALO), "row", ahead)
    bottom = lax.ppermute(edge_rows(0), "row", back)
    maps = jnp.transpose(inputs[0], (1, 0, 2))
    tags = jnp.transpose(tags, (1, 0, 2))
    params = pltpu.CompilerParams(vmem_limit_bytes=56 << 20)
    pack = jax.ShapeDtypeStruct((CHANNELS, 128), BF)
    start = jax.ShapeDtypeStruct((CHANNELS, WIDTH), BF)
    left_edge, right_edge, start = pl.pallas_call(
        edges_kernel, out_shape=(pack, pack, start), compiler_params=params
    )(maps, tags)
    pack = jax.ShapeDtypeStruct((CHANNELS, 256), BF)
    left_edge, right_edge = pl.pallas_call(
        corners_kernel, out_shape=(pack, pack), compiler_params=params
    )(left_edge, right_edge, top, bottom)
    left = lax.ppermute(right_edge, "col", ahead)
    right = lax.ppermute(left_edge, "col", back)

    w2 = jnp.transpose(spatial_weight, (0, 2, 1, 3)).reshape(3 * MID, 3 * MID)
    w2t = jnp.transpose(spatial_weight, (0, 3, 1, 2)).reshape(3 * MID, 3 * MID)
    w3 = jnp.pad(class_weight, ((0, 0), (0, 0), (0, 136 - OUT), (0, 0)))
    w3 = jnp.transpose(w3, (0, 2, 1, 3)).reshape(3 * 136, 3 * C)
    w9 = class_weight.reshape(9, OUT, C)
    w3t = jnp.concatenate(
        [
            w9[:, :128].reshape(9 * 128, C),
            jnp.pad(w9[:, 128:], ((0, 0), (0, TAIL - 7), (0, 0))).reshape(9 * TAIL, C),
            jnp.zeros((8, C), BF),
        ],
        axis=0,
    ).T
    spread = np.zeros((136, CHANNELS - C), np.float32)
    for o in range(OUT):
        spread[o, o // K] = 1.0
        spread[o, A + o // K] = 16.0
    spread = jnp.asarray(spread, BF)

    shape = jax.ShapeDtypeStruct
    out = pl.pallas_call(
        main_kernel,
        out_shape=shape((DEVICES * SHARE, 128), BF),
        in_specs=[pl.BlockSpec(memory_space=pl.ANY)] + [pl.BlockSpec(memory_space=pltpu.VMEM)] * 12,
        scratch_shapes=[
            pltpu.VMEM((CHANNELS, WIDTH), BF),
            pltpu.VMEM((MID, WIDTH), BF),
            pltpu.VMEM((MID, WIDTH), BF),
            pltpu.VMEM((C, WIDTH), BF),
            pltpu.VMEM((128, WIDTH), BF),
            pltpu.VMEM((TAIL, WIDTH), F32),
            pltpu.VMEM((MID, WIDTH), BF),
            pltpu.VMEM((3 * 136, WIDTH), F32),
            pltpu.VMEM((8, 128), F32),
            pltpu.VMEM((8, 128), F32),
            pltpu.VMEM((STACK, C), F32),
            pltpu.VMEM((MID, C), F32),
            pltpu.VMEM((3 * MID, 3 * MID), F32),
            pltpu.VMEM((MID, C), F32),
            pltpu.SemaphoreType.DMA(()),
        ],
        compiler_params=params,
    )(
        start, top, bottom, left, right,
        reduce_weight, w2, w2t, expand_weight, expand_weight.T, w3, w3t, spread,
    )

    sent = out.reshape(DEVICES, SHARE, 128)
    came = lax.all_to_all(sent, ALL, 0, 0, tiled=True)
    index = lax.axis_index(ALL).astype(jnp.int32).reshape(1)
    copies = pl.pallas_call(
        sum_kernel,
        out_shape=shape((DEVICES, SHARE, 128), BF),
        in_specs=[
            pl.BlockSpec(memory_space=pltpu.SMEM),
            pl.BlockSpec(memory_space=pltpu.VMEM),
        ],
        compiler_params=params,
    )(index, came)
    flat = lax.all_to_all(copies, ALL, 0, 0, tiled=True).reshape(DEVICES * SHARE, 128)
    loss, gred, gspat, gexp, gclass = pl.pallas_call(
        final_kernel,
        out_shape=(
            shape((1, 1), F32),
            shape((MID, C), F32),
            shape((9, MID, MID), F32),
            shape((MID, C), F32),
            shape((9, OUT, C), F32),
        ),
        compiler_params=params,
    )(flat)
    return (
        loss.reshape(()),
        gred,
        gspat.reshape(3, 3, MID, MID),
        gexp.T,
        gclass.reshape(3, 3, OUT, C),
    )


def solution(mesh):
    maps = P("dp", None, "row", "col")
    return jax.shard_map(
        per_device,
        mesh=mesh,
        in_specs=(maps, P(), P(), P(), P(), maps, maps),
        out_specs=(P(), P(), P(), P(), P()),
        check_vma=False,
    )
```

```python
import jax
import jax.numpy as jnp
import numpy as np
from jax import lax
from jax.experimental import pallas as pl
from jax.experimental.pallas import tpu as pltpu
from jax.sharding import Mesh
from jax.sharding import PartitionSpec as P

A = 9
K = 15
OUT = A * K
C = 256
MID = 64
HALO = 4
ROWS = 32
COLS = 128
FULL = ROWS + 2 * HALO
STRIDE = COLS + 2 * HALO
CHANNELS = 288
MARGIN = 256
WIDTH = 6656
RIGHT = MARGIN + 5120
PIPE = 640
SPLIT = (
    (0, 2816, 2),
    (0, 2816, 2),
    (128, 2688, 2),
    (0, PIPE, 9),
    (256, PIPE, 8),
    (384, 2432, 2),
    (384, 2432, 2),
    (512, 2304, 2),
)
LABEL0 = C
MASK0 = C + A
ONE0 = C + 2 * A
TAGS = CHANNELS - C
TAIL = 8
STACK = 9 * 128 + 9 * TAIL + 8
CHIPS = ("y", "row", "col")
DEVICES = 128
PAIRS = 64
SHARE = 24
HALF = PAIRS * SHARE
RED0 = 2 * STACK
SPAT0 = RED0 + 2 * MID
EXP0 = SPAT0 + 9 * MID // 2
STAT0 = EXP0 + C // 2
TAPS = [(dy - 1) * STRIDE + (dx - 1) for dy in range(3) for dx in range(3)]
BF = jnp.bfloat16
F32 = jnp.float32


def put(ref, rows, tile, value, lo, hi):
    lane = lax.broadcasted_iota(jnp.int32, value.shape, 1)
    where = slice(tile * 128, tile * 128 + 128)
    ref[rows, where] = jnp.where((lane >= lo) & (lane < hi), value, ref[rows, where])


BODY = slice(0, C)
REST = slice(C, CHANNELS)
BOTH = slice(0, CHANNELS)


def place(ref, rows, source, r):
    at = MARGIN + r * STRIDE + HALO
    turn, tile = (at % 128, at // 128)
    turned = pltpu.roll(source, turn, 1)
    put(ref, rows, tile, turned, turn, 128)
    put(ref, rows, tile + 1, turned, 0, turn)


def edges_kernel(maps_ref, tags_ref, left_ref, right_ref, x_ref):
    x_ref[...] = jnp.zeros_like(x_ref)
    left_ref[...] = jnp.zeros_like(left_ref)
    right_ref[...] = jnp.zeros_like(right_ref)
    for r in range(ROWS):
        at = HALO * r
        for rows, source in ((BODY, maps_ref[r]), (REST, tags_ref[r])):
            put(left_ref, rows, 0, pltpu.roll(source, at, 1), at, at + HALO)
            put(right_ref, rows, 0, pltpu.roll(source, (at + HALO) % 128, 1), at, at + HALO)
            place(x_ref, rows, source, r + HALO)


def corners_kernel(left_ref, right_ref, top_ref, bottom_ref, wide_left_ref, wide_right_ref):
    for edge_ref, wide_ref in ((left_ref, wide_left_ref), (right_ref, wide_right_ref)):
        wide_ref[:, :128] = edge_ref[...]
        wide_ref[:, 128:] = jnp.zeros_like(edge_ref)
    for h in range(2 * HALO):
        source = top_ref[h] if h < HALO else bottom_ref[h - HALO]
        at = HALO * h
        put(wide_left_ref, BOTH, 1, pltpu.roll(source, at, 1), at, at + HALO)
        put(wide_right_ref, BOTH, 1, pltpu.roll(source, at + HALO, 1), at, at + HALO)


def aligned(lane):
    return lane if isinstance(lane, int) else pl.multiple_of(lane, 128)


def window(ref, rows, lane, shift, n):
    base = (shift // 128) * 128
    turn = shift - base
    if turn == 0:
        return ref[rows, pl.ds(aligned(lane + base), n)]
    wide = ref[rows, pl.ds(aligned(lane + base), n + 128)]
    return pltpu.roll(wide, n + 128 - turn, 1)[:, :n]


def interior(lane, shift, n):
    p = lane - MARGIN + shift + lax.broadcasted_iota(jnp.int32, (1, n), 1)
    r = (p * 30841) >> 22
    c = p - r * STRIDE
    return (r >= HALO) & (r < HALO + ROWS) & (c >= HALO) & (c < HALO + COLS)


def masked(value, mask):
    return value * jnp.where(mask, 1.0, 0.0).astype(BF)


def dot(a, b):
    return jnp.dot(a, b, preferred_element_type=F32)


def dot_nt(a, b):
    return lax.dot_general(a, b, (((1,), (1,)), ((), ())), preferred_element_type=F32)


def chunks(start, n, count, body):
    def step(j, carry):
        body(pl.multiple_of(MARGIN + start + j * n, 128), n)
        return carry

    lax.fori_loop(0, count, step, 0)


def across(ref, lane, sign, n):
    return jnp.concatenate([window(ref, slice(None), lane, sign * k, n) for k in (-1, 0, 1)], axis=0)


def down(ref, lane, sign, size, n):
    parts = [
        window(ref, slice(k * size, k * size + size), lane, sign * (k - 1) * STRIDE, n)
        for k in range(3)
    ]
    return parts[0] + parts[1] + parts[2]


def main_kernel(
    core_ref, x0_ref, top_ref, bottom_ref, left_ref, right_ref,
    wr_ref, w2_ref, w2t_ref, we_ref, wet_ref, w3_ref, w3t_ref, e_ref,
    keep_ref, send_ref,
    x_ref, first_ref, second_ref, block_ref, d_ref, dt_ref, ds_ref, p_ref, facc_ref, cacc_ref,
    gclass_ref, gred_ref, gspat_ref, gexp_ref, out_ref, sem,
):
    copy = pltpu.make_async_copy(x0_ref, x_ref, sem)
    copy.start()
    for ref in (first_ref, second_ref, block_ref, d_ref, dt_ref, ds_ref, p_ref):
        ref[:, : 2 * MARGIN] = jnp.zeros((ref.shape[0], 2 * MARGIN), ref.dtype)
        ref[:, RIGHT:] = jnp.zeros((ref.shape[0], WIDTH - RIGHT), ref.dtype)
    for ref in (gclass_ref, gred_ref, gspat_ref, gexp_ref, facc_ref, cacc_ref):
        ref[...] = jnp.zeros_like(ref)
    copy.wait()
    for r in range(FULL):
        if r < HALO:
            place(x_ref, BOTH, top_ref[r], r)
        elif r >= HALO + ROWS:
            place(x_ref, BOTH, bottom_ref[r - HALO - ROWS], r)
        if HALO <= r < HALO + ROWS:
            spot = HALO * (r - HALO)
        else:
            spot = 128 + HALO * (r if r < HALO else r - ROWS)
        source = slice(spot // 128 * 128, spot // 128 * 128 + 128)
        for edge_ref, at in ((left_ref, MARGIN + r * STRIDE), (right_ref, MARGIN + r * STRIDE + HALO + COLS)):
            turned = pltpu.roll(edge_ref[:, source], (at - spot) % 128, 1)
            put(x_ref, BOTH, at // 128, turned, at % 128, at % 128 + HALO)

    def first_step(lane, n):
        x = x_ref[:C, pl.ds(lane, n)]
        first_ref[:, pl.ds(lane, n)] = jnp.maximum(dot(wr_ref[...], x), 0.0).astype(BF)

    chunks(*SPLIT[0], first_step)

    def spatial_step(lane, n):
        p_ref[: 3 * MID, pl.ds(lane, n)] = dot(w2_ref[...], across(first_ref, lane, 1, n))

    chunks(*SPLIT[1], spatial_step)

    def block_step(lane, n):
        here = pl.ds(lane, n)
        second = jnp.maximum(down(p_ref, lane, 1, MID, n), 0.0)
        inside = x_ref[ONE0 - 2 : ONE0 + 14, here].astype(F32)[2:3]
        second = jnp.where(inside > 0.5, second, 0.0).astype(BF)
        second_ref[:, here] = second
        total = x_ref[:C, here].astype(F32) + dot(we_ref[...], second)
        block_ref[:, here] = jnp.maximum(total, 0.0).astype(BF)

    chunks(*SPLIT[2], block_step)

    def class_step(lane, n):
        p_ref[:, pl.ds(lane, n)] = dot(w3_ref[...], across(block_ref, lane, 1, n))

    channel = lax.broadcasted_iota(jnp.int32, (136, 1), 0)
    wanted = (channel - 15 * ((channel * 4370) >> 16) + 17).astype(F32)

    def focal_step(lane, n):
        here = pl.ds(lane, n)
        z = down(p_ref, lane, 1, 136, n)
        tags = x_ref[C:CHANNELS, here]
        code = dot(e_ref[...], tags)
        target = code == wanted
        counted = code > 15.5
        u = jnp.where(target, z, -z)
        alpha = jnp.where(target, 0.25, 0.75)
        e = jnp.exp(-jnp.abs(u))
        d = 1.0 / (1.0 + e)
        ed = e * d
        positive = u >= 0
        p = jnp.where(positive, ed, d)
        q = jnp.where(positive, d, ed)
        ls = jnp.minimum(u, 0.0) - jnp.log1p(e)
        ap2 = jnp.where(counted, alpha, 0.0) * p * p
        grad = ap2 * (2.0 * q * ls - p)
        grad = jnp.where(target, grad, -grad)
        d_ref[:, here] = grad[:128].astype(BF)
        dt_ref[:, here] = grad[128:].astype(BF).astype(F32)
        inner = interior(lane, 0, n)
        focal = jnp.where(inner, ap2 * ls, 0.0)
        facc_ref[...] -= jnp.sum(focal.reshape(17, 8, n), axis=0)
        labels = tags[:16].astype(F32)
        tag = lax.broadcasted_iota(jnp.int32, (16, n), 0)
        positives = jnp.where((labels > 0.5) & (tag < A) & inner, 1.0, 0.0)
        cacc_ref[...] += positives[:8] + positives[8:]

    begin, n, count = SPLIT[3]
    for j in range(count + 2):
        if j >= 2 and j - 2 < SPLIT[4][2]:
            for k in range(0, n, 128):
                focal_step(MARGIN + SPLIT[4][0] + (j - 2) * n + k, 128)
        if j < count:
            class_step(MARGIN + begin + j * n, n)

    def class_back(lane, n):
        here = pl.ds(lane, n)
        mains = [window(d_ref, slice(None), lane, -s, n) for s in TAPS]
        tails = [window(dt_ref, slice(None), lane, -s, n) for s in TAPS]
        inner = [interior(lane, -s, n) for s in TAPS]
        spare = jnp.zeros((8, n), F32)
        block = block_ref[:, here]
        stack = jnp.concatenate(
            mains + [jnp.concatenate(tails + [spare], axis=0).astype(BF)], axis=0
        )
        dblock = dot(w3t_ref[...], stack)
        dsum = jnp.where(block.astype(F32) > 0, dblock, 0.0).astype(BF)
        second = second_ref[:, here]
        within = interior(lane, 0, n)
        gexp_ref[...] += dot_nt(masked(second, within), dsum)
        dsecond = jnp.where(second.astype(F32) > 0, dot(wet_ref[...], dsum), 0.0)
        ds_ref[:, here] = dsecond.astype(BF)
        own = jnp.concatenate(
            [masked(m, i) for m, i in zip(mains, inner)]
            + [
                jnp.concatenate(
                    [jnp.where(i, t, 0.0) for t, i in zip(tails, inner)] + [spare], axis=0
                ).astype(BF)
            ],
            axis=0,
        )
        gclass_ref[...] += dot_nt(own, block)

    chunks(*SPLIT[5], class_back)

    def spatial_back(lane, n):
        stack = across(ds_ref, lane, -1, n)
        p_ref[: 3 * MID, pl.ds(lane, n)] = dot(w2t_ref[...], stack)
        own = jnp.concatenate(
            [
                masked(stack[k * MID : k * MID + MID], interior(lane, 1 - k, n))
                for k in range(3)
            ],
            axis=0,
        )
        first = jnp.concatenate(
            [window(first_ref, slice(None), lane, k * STRIDE, n) for k in (-1, 0, 1)], axis=0
        )
        gspat_ref[...] += dot_nt(own, first)

    chunks(*SPLIT[6], spatial_back)

    def first_back(lane, n):
        here = pl.ds(lane, n)
        dfirst = down(p_ref, lane, -1, MID, n)
        keep = (first_ref[:, here].astype(F32) > 0) & interior(lane, 0, n)
        dfirst = jnp.where(keep, dfirst, 0.0).astype(BF)
        gred_ref[...] += dot_nt(dfirst, x_ref[:C, here])

    chunks(*SPLIT[7], first_back)

    out_ref[:STACK] = gclass_ref[:, :128].astype(BF)
    out_ref[STACK:RED0] = gclass_ref[:, 128:].astype(BF)
    out_ref[RED0 : RED0 + MID] = gred_ref[:, :128].astype(BF)
    out_ref[RED0 + MID : SPAT0] = gred_ref[:, 128:].astype(BF)
    out_ref[SPAT0 : SPAT0 + 3 * MID] = gspat_ref[:, : 2 * MID].astype(BF)
    half = 3 * MID // 2
    out_ref[SPAT0 + 3 * MID : EXP0] = jnp.concatenate(
        [gspat_ref[:half, 2 * MID :], gspat_ref[half:, 2 * MID :]], axis=1
    ).astype(BF)
    out_ref[EXP0 : EXP0 + MID] = gexp_ref[:, :128].astype(BF)
    out_ref[EXP0 + MID : STAT0] = gexp_ref[:, 128:].astype(BF)
    out_ref[STAT0:] = jnp.zeros((DEVICES * SHARE - STAT0, 128), BF)
    focal = jnp.sum(facc_ref[...], keepdims=True)
    count = jnp.sum(cacc_ref[...], keepdims=True)
    stats = stat_rows(focal, count, 16)
    at = lax.broadcasted_iota(jnp.int32, (16, 128), 0)
    out_ref[STAT0 : STAT0 + 16] = jnp.where(at == core_ref[0], stats, 0.0).astype(BF)
    for ref, core in ((keep_ref, core_ref[0]), (send_ref, 1 - core_ref[0])):
        ref[...] = out_ref[pl.ds(pl.multiple_of(core * HALF, HALF), HALF), :]


def rounded(x):
    return x.astype(BF).astype(F32)


def stat_rows(focal, count, rows):
    lane = lax.broadcasted_iota(jnp.int32, (rows, 128), 1)
    out = jnp.zeros((rows, 128), F32)
    for at, value in ((0, focal), (3, count)):
        value = jnp.broadcast_to(value, (rows, 128))
        for k in range(3):
            piece = rounded(value)
            out = jnp.where(lane == at + k, piece, out)
            value = value - piece
    return out


def stat_values(row):
    lane = lax.broadcasted_iota(jnp.int32, row.shape, 1)
    focal = jnp.sum(jnp.where(lane < 3, row, 0.0), axis=1, keepdims=True)
    count = jnp.sum(jnp.where((lane >= 3) & (lane < 6), row, 0.0), axis=1, keepdims=True)
    return focal, count


def sum_kernel(index_ref, came_ref, copies_ref):
    total = came_ref[0].astype(F32)
    for k in range(1, PAIRS):
        total = total + came_ref[k].astype(F32)
    row = STAT0 % SHARE
    at = lax.broadcasted_iota(jnp.int32, (SHARE, 128), 0)
    focal, count = stat_values(total[row : row + 1] + total[row + 1 : row + 2])
    stats = stat_rows(focal, count, SHARE)
    total = jnp.where((at == row) & (index_ref[0] == STAT0 // SHARE), stats, total)
    total = total.astype(BF)
    for k in range(PAIRS):
        copies_ref[k] = total


def final_kernel(
    core_ref, own_ref, other_ref, loss_ref, gred_ref, gspat_ref, gexp_ref, gclass_ref, flat_ref
):
    for ref, core in ((own_ref, core_ref[0]), (other_ref, 1 - core_ref[0])):
        flat_ref[pl.ds(pl.multiple_of(core * HALF, HALF), HALF), :] = ref[...]
    focal, count = stat_values(flat_ref[STAT0 : STAT0 + 16].astype(F32)[:1])
    scale = 1.0 / count
    loss_ref[...] = focal * scale

    def rows(lo, n):
        return flat_ref[lo : lo + n].astype(F32) * scale

    for half in range(2):
        lanes = slice(half * 128, half * 128 + 128)
        tails = rows(half * STACK + 9 * 128, STACK - 9 * 128)
        for t in range(9):
            gclass_ref[t, :128, lanes] = rows(half * STACK + t * 128, 128)
            gclass_ref[t, 128:, lanes] = tails[t * TAIL : t * TAIL + 7]
        gred_ref[:, lanes] = rows(RED0 + half * MID, MID)
        gexp_ref[:, lanes] = rows(EXP0 + half * MID, MID)
    spat = rows(SPAT0, 3 * MID)
    last = rows(SPAT0 + 3 * MID, 3 * MID // 2)
    half = 3 * MID // 2
    for dx in range(3):
        for dy in range(2):
            gspat_ref[3 * dy + dx] = spat[dx * MID : dx * MID + MID, dy * MID : dy * MID + MID]
    gspat_ref[6] = last[:MID, :MID]
    gspat_ref[7, : half - MID] = last[MID:, :MID]
    gspat_ref[7, half - MID :] = last[: 2 * MID - half, MID:]
    gspat_ref[8] = last[2 * MID - half :, MID:]


def per_device(
    inputs, reduce_weight, spatial_weight, expand_weight, class_weight, anchor_labels, anchor_mask
):
    one = jnp.ones((1, ROWS, COLS), BF)
    none = jnp.zeros((TAGS - 2 * A - 1, ROWS, COLS), BF)
    tags = jnp.concatenate(
        [anchor_labels[0].astype(BF), anchor_mask[0].astype(BF), one, none], axis=0
    )

    def edge_rows(at):
        fields = jnp.concatenate([inputs[0, :, at : at + HALO], tags[:, at : at + HALO]], axis=0)
        return jnp.transpose(fields, (1, 0, 2))

    ahead = [(i, i + 1) for i in range(3)]
    back = [(i + 1, i) for i in range(3)]
    top = lax.ppermute(edge_rows(ROWS - HALO), "row", ahead)
    bottom = lax.ppermute(edge_rows(0), "row", back)
    maps = jnp.transpose(inputs[0], (1, 0, 2))
    tags = jnp.transpose(tags, (1, 0, 2))
    params = pltpu.CompilerParams(vmem_limit_bytes=56 << 20)
    pack = jax.ShapeDtypeStruct((CHANNELS, 128), BF)
    start = jax.ShapeDtypeStruct((CHANNELS, WIDTH), BF)
    left_edge, right_edge, start = pl.pallas_call(
        edges_kernel, out_shape=(pack, pack, start), compiler_params=params
    )(maps, tags)
    pack = jax.ShapeDtypeStruct((CHANNELS, 256), BF)
    left_edge, right_edge = pl.pallas_call(
        corners_kernel, out_shape=(pack, pack), compiler_params=params
    )(left_edge, right_edge, top, bottom)
    left = lax.ppermute(right_edge, "col", ahead)
    right = lax.ppermute(left_edge, "col", back)

    w2 = jnp.transpose(spatial_weight, (0, 2, 1, 3)).reshape(3 * MID, 3 * MID)
    w2t = jnp.transpose(spatial_weight, (0, 3, 1, 2)).reshape(3 * MID, 3 * MID)
    w3 = jnp.pad(class_weight, ((0, 0), (0, 0), (0, 136 - OUT), (0, 0)))
    w3 = jnp.transpose(w3, (0, 2, 1, 3)).reshape(3 * 136, 3 * C)
    w9 = class_weight.reshape(9, OUT, C)
    w3t = jnp.concatenate(
        [
            w9[:, :128].reshape(9 * 128, C),
            jnp.pad(w9[:, 128:], ((0, 0), (0, TAIL - 7), (0, 0))).reshape(9 * TAIL, C),
            jnp.zeros((8, C), BF),
        ],
        axis=0,
    ).T
    spread = np.zeros((136, CHANNELS - C), np.float32)
    for o in range(OUT):
        spread[o, o // K] = 1.0
        spread[o, A + o // K] = 16.0
    spread = jnp.asarray(spread, BF)

    shape = jax.ShapeDtypeStruct
    core = lax.axis_index("core").astype(jnp.int32).reshape(1)
    keep, send = pl.pallas_call(
        main_kernel,
        out_shape=(shape((HALF, 128), BF), shape((HALF, 128), BF)),
        in_specs=[pl.BlockSpec(memory_space=pltpu.SMEM), pl.BlockSpec(memory_space=pl.ANY)] + [pl.BlockSpec(memory_space=pltpu.VMEM)] * 12,
        scratch_shapes=[
            pltpu.VMEM((CHANNELS, WIDTH), BF),
            pltpu.VMEM((MID, WIDTH), BF),
            pltpu.VMEM((MID, WIDTH), BF),
            pltpu.VMEM((C, WIDTH), BF),
            pltpu.VMEM((128, WIDTH), BF),
            pltpu.VMEM((TAIL, WIDTH), F32),
            pltpu.VMEM((MID, WIDTH), BF),
            pltpu.VMEM((3 * 136, WIDTH), F32),
            pltpu.VMEM((8, 128), F32),
            pltpu.VMEM((8, 128), F32),
            pltpu.VMEM((STACK, C), F32),
            pltpu.VMEM((MID, C), F32),
            pltpu.VMEM((3 * MID, 3 * MID), F32),
            pltpu.VMEM((MID, C), F32),
            pltpu.VMEM((DEVICES * SHARE, 128), BF),
            pltpu.SemaphoreType.DMA(()),
        ],
        compiler_params=params,
    )(
        core, start, top, bottom, left, right,
        reduce_weight, w2, w2t, expand_weight, expand_weight.T, w3, w3t, spread,
    )

    swap = [(0, 1), (1, 0)]
    pair = lax.ppermute(send, "core", swap).astype(F32) + keep.astype(F32)
    came = lax.all_to_all(pair.astype(BF).reshape(PAIRS, SHARE, 128), CHIPS, 0, 0, tiled=True)
    index = core * PAIRS + lax.axis_index(CHIPS).astype(jnp.int32)
    copies = pl.pallas_call(
        sum_kernel,
        out_shape=shape((PAIRS, SHARE, 128), BF),
        in_specs=[
            pl.BlockSpec(memory_space=pltpu.SMEM),
            pl.BlockSpec(memory_space=pltpu.VMEM),
        ],
        compiler_params=params,
    )(index, came)
    own = lax.all_to_all(copies, CHIPS, 0, 0, tiled=True).reshape(PAIRS * SHARE, 128)
    other = lax.ppermute(own, "core", swap)
    loss, gred, gspat, gexp, gclass = pl.pallas_call(
        final_kernel,
        out_shape=(
            shape((1, 1), F32),
            shape((MID, C), F32),
            shape((9, MID, MID), F32),
            shape((MID, C), F32),
            shape((9, OUT, C), F32),
        ),
        in_specs=[pl.BlockSpec(memory_space=pltpu.SMEM)]
        + [pl.BlockSpec(memory_space=pltpu.VMEM)] * 2,
        scratch_shapes=[pltpu.VMEM((DEVICES * SHARE, 128), BF)],
        compiler_params=params,
    )(core, own, other)
    return (
        loss.reshape(()),
        gred,
        gspat.reshape(3, 3, MID, MID),
        gexp.T,
        gclass.reshape(3, 3, OUT, C),
    )


def solution(mesh):
    finer = Mesh(
        mesh.devices.reshape(4, 2, mesh.shape["row"], mesh.shape["col"]),
        ("y", "core", "row", "col"),
    )
    maps = P(("y", "core"), None, "row", "col")
    return jax.shard_map(
        per_device,
        mesh=finer,
        in_specs=(maps, P(), P(), P(), P(), maps, maps),
        out_specs=(P(), P(), P(), P(), P()),
        check_vma=False,
    )
```

```python
import jax
import jax.numpy as jnp
import numpy as np
from jax import lax
from jax.experimental import pallas as pl
from jax.experimental.pallas import tpu as pltpu
from jax.sharding import Mesh
from jax.sharding import PartitionSpec as P

A = 9
K = 15
OUT = A * K
C = 256
MID = 64
HALO = 4
ROWS = 32
COLS = 128
FULL = ROWS + 2 * HALO
STRIDE = COLS + 2 * HALO
CHANNELS = 288
MARGIN = 256
WIDTH = 6656
RIGHT = MARGIN + 5120
PIPE = 640
SPLIT = (
    (0, 2816, 2),
    (0, 2816, 2),
    (128, 2688, 2),
    (0, PIPE, 9),
    (256, PIPE, 8),
    (384, 2432, 2),
    (384, 2432, 2),
    (512, 2304, 2),
)
LABEL0 = C
MASK0 = C + A
ONE0 = C + 2 * A
TAGS = CHANNELS - C
TAIL = 8
STACK = 9 * 128 + 9 * TAIL + 8
CHIPS = ("y", "row", "col")
DEVICES = 128
PAIRS = 64
SHARE = 24
HALF = PAIRS * SHARE
RED0 = 2 * STACK
SPAT0 = RED0 + 2 * MID
EXP0 = SPAT0 + 9 * MID // 2
STAT0 = EXP0 + C // 2
TAPS = [(dy - 1) * STRIDE + (dx - 1) for dy in range(3) for dx in range(3)]
BF = jnp.bfloat16
F32 = jnp.float32


def put(ref, rows, tile, value, lo, hi):
    lane = lax.broadcasted_iota(jnp.int32, value.shape, 1)
    where = slice(tile * 128, tile * 128 + 128)
    ref[rows, where] = jnp.where((lane >= lo) & (lane < hi), value, ref[rows, where])


BODY = slice(0, C)
REST = slice(C, CHANNELS)
BOTH = slice(0, CHANNELS)


def place(ref, rows, source, r):
    at = MARGIN + r * STRIDE + HALO
    turn, tile = (at % 128, at // 128)
    turned = pltpu.roll(source, turn, 1)
    put(ref, rows, tile, turned, turn, 128)
    put(ref, rows, tile + 1, turned, 0, turn)


def put_span(ref, value, at, width):
    tile, low = divmod(at, 128)
    put(ref, BOTH, tile, value, low, min(low + width, 128))
    if low + width > 128:
        put(ref, BOTH, tile + 1, value, 0, low + width - 128)


def spot(r):
    if HALO <= r < HALO + ROWS:
        return HALO * (r - HALO)
    return 128 + HALO * (r if r < HALO else r - ROWS)


def edges_kernel(maps_ref, tags_ref, left_ref, right_ref, x_ref):
    x_ref[...] = jnp.zeros_like(x_ref)
    left_ref[...] = jnp.zeros_like(left_ref)
    right_ref[...] = jnp.zeros_like(right_ref)
    for r in range(ROWS):
        at = HALO * r
        for rows, source in ((BODY, maps_ref[r]), (REST, tags_ref[r])):
            put(left_ref, rows, 0, pltpu.roll(source, at, 1), at, at + HALO)
            put(right_ref, rows, 0, pltpu.roll(source, (at + HALO) % 128, 1), at, at + HALO)
            place(x_ref, rows, source, r + HALO)


def corners_kernel(left_ref, right_ref, top_ref, bottom_ref, wide_left_ref, wide_right_ref):
    for edge_ref, wide_ref in ((left_ref, wide_left_ref), (right_ref, wide_right_ref)):
        wide_ref[:, :128] = edge_ref[...]
        wide_ref[:, 128:] = jnp.zeros_like(edge_ref)
    for h in range(2 * HALO):
        source = top_ref[h] if h < HALO else bottom_ref[h - HALO]
        at = HALO * h
        put(wide_left_ref, BOTH, 1, pltpu.roll(source, at, 1), at, at + HALO)
        put(wide_right_ref, BOTH, 1, pltpu.roll(source, at + HALO, 1), at, at + HALO)


def aligned(lane):
    return lane if isinstance(lane, int) else pl.multiple_of(lane, 128)


def window(ref, rows, lane, shift, n):
    base = (shift // 128) * 128
    turn = shift - base
    if turn == 0:
        return ref[rows, pl.ds(aligned(lane + base), n)]
    wide = ref[rows, pl.ds(aligned(lane + base), n + 128)]
    return pltpu.roll(wide, n + 128 - turn, 1)[:, :n]


def interior(lane, shift, n):
    p = lane - MARGIN + shift + lax.broadcasted_iota(jnp.int32, (1, n), 1)
    r = (p * 30841) >> 22
    c = p - r * STRIDE
    return (r >= HALO) & (r < HALO + ROWS) & (c >= HALO) & (c < HALO + COLS)


def masked(value, mask):
    return value * jnp.where(mask, 1.0, 0.0).astype(BF)


def dot(a, b):
    return jnp.dot(a, b, preferred_element_type=F32)


def dot_nt(a, b):
    return lax.dot_general(a, b, (((1,), (1,)), ((), ())), preferred_element_type=F32)


def chunks(start, n, count, body):
    def step(j, carry):
        body(pl.multiple_of(MARGIN + start + j * n, 128), n)
        return carry

    lax.fori_loop(0, count, step, 0)


def across(ref, lane, sign, n):
    return jnp.concatenate([window(ref, slice(None), lane, sign * k, n) for k in (-1, 0, 1)], axis=0)


def down(ref, lane, sign, size, n):
    parts = [
        window(ref, slice(k * size, k * size + size), lane, sign * (k - 1) * STRIDE, n)
        for k in range(3)
    ]
    return parts[0] + parts[1] + parts[2]


def main_kernel(
    core_ref, x0_ref, top_ref, bottom_ref, left_ref, right_ref,
    wr_ref, w2_ref, w2t_ref, we_ref, wet_ref, w3_raw, w3t_raw, e_ref,
    keep_ref, send_ref,
    x_ref, first_ref, second_ref, block_ref, d_ref, dt_ref, ds_ref, p_ref, facc_ref, cacc_ref,
    gclass_ref, gred_ref, gspat_ref, gexp_ref, out_ref, w3_ref, w3t_ref, sem,
):
    copy = pltpu.make_async_copy(x0_ref, x_ref, sem.at[0])
    weights = pltpu.make_async_copy(w3_raw, w3_ref, sem.at[1])
    weights_back = pltpu.make_async_copy(w3t_raw, w3t_ref, sem.at[2])
    for each in (copy, weights, weights_back):
        each.start()
    p_ref[:, :MARGIN] = jnp.zeros((p_ref.shape[0], MARGIN), F32)
    for ref in (first_ref, second_ref, block_ref, d_ref, dt_ref, ds_ref):
        ref[:, : 2 * MARGIN] = jnp.zeros((ref.shape[0], 2 * MARGIN), ref.dtype)
        ref[:, RIGHT:] = jnp.zeros((ref.shape[0], WIDTH - RIGHT), ref.dtype)
    for ref in (gclass_ref, gred_ref, gspat_ref, gexp_ref, facc_ref, cacc_ref):
        ref[...] = jnp.zeros_like(ref)
    copy.wait()
    for h in range(HALO):
        place(x_ref, BOTH, top_ref[h], h)
        place(x_ref, BOTH, bottom_ref[h], h + HALO + ROWS)
    lane = lax.broadcasted_iota(jnp.int32, (CHANNELS, 128), 1)
    for r in range(-1, FULL):
        at = MARGIN + r * STRIDE + HALO + COLS
        if 0 <= r < FULL - 1 and spot(r + 1) == spot(r) + HALO:
            tile, low = divmod(spot(r), 128)
            where = slice(tile * 128, tile * 128 + 128)
            both = jnp.where(lane < low + HALO, right_ref[:, where], left_ref[:, where])
            put_span(x_ref, pltpu.roll(both, (at - low) % 128, 1), at, 2 * HALO)
            continue
        for ref, row, to in ((right_ref, r, at), (left_ref, r + 1, at + HALO)):
            if 0 <= row < FULL:
                tile, low = divmod(spot(row), 128)
                one = ref[:, tile * 128 : tile * 128 + 128]
                put_span(x_ref, pltpu.roll(one, (to - low) % 128, 1), to, HALO)

    def first_step(lane, n):
        x = x_ref[:C, pl.ds(lane, n)]
        first_ref[:, pl.ds(lane, n)] = jnp.maximum(dot(wr_ref[...], x), 0.0).astype(BF)

    chunks(*SPLIT[0], first_step)

    def spatial_step(lane, n):
        p_ref[: 3 * MID, pl.ds(lane, n)] = dot(w2_ref[...], across(first_ref, lane, 1, n))

    chunks(*SPLIT[1], spatial_step)

    def block_step(lane, n):
        here = pl.ds(lane, n)
        second = jnp.maximum(down(p_ref, lane, 1, MID, n), 0.0)
        inside = x_ref[ONE0 - 2 : ONE0 + 14, here].astype(F32)[2:3]
        second = jnp.where(inside > 0.5, second, 0.0).astype(BF)
        second_ref[:, here] = second
        total = x_ref[:C, here].astype(F32) + dot(we_ref[...], second)
        block_ref[:, here] = jnp.maximum(total, 0.0).astype(BF)

    chunks(*SPLIT[2], block_step)

    def class_step(lane, n):
        p_ref[:, pl.ds(lane, n)] = dot(w3_ref[...], across(block_ref, lane, 1, n))

    channel = lax.broadcasted_iota(jnp.int32, (136, 1), 0)
    wanted = (channel - 15 * ((channel * 4370) >> 16) + 17).astype(F32)

    def focal_step(lane, n):
        here = pl.ds(lane, n)
        z = down(p_ref, lane, 1, 136, n)
        tags = x_ref[C:CHANNELS, here]
        code = dot(e_ref[...], tags)
        target = code == wanted
        counted = code > 15.5
        u = jnp.where(target, z, -z)
        alpha = jnp.where(target, 0.25, 0.75)
        e = jnp.exp(-jnp.abs(u))
        d = 1.0 / (1.0 + e)
        ed = e * d
        positive = u >= 0
        p = jnp.where(positive, ed, d)
        q = jnp.where(positive, d, ed)
        ls = jnp.minimum(u, 0.0) - jnp.log1p(e)
        ap2 = jnp.where(counted, alpha, 0.0) * p * p
        grad = ap2 * (2.0 * q * ls - p)
        grad = jnp.where(target, grad, -grad)
        d_ref[:, here] = grad[:128].astype(BF)
        dt_ref[:, here] = grad[128:].astype(BF).astype(F32)
        inner = interior(lane, 0, n)
        focal = jnp.where(inner, ap2 * ls, 0.0)
        facc_ref[...] -= jnp.sum(focal.reshape(17, 8, n), axis=0)
        labels = tags[:16].astype(F32)
        tag = lax.broadcasted_iota(jnp.int32, (16, n), 0)
        positives = jnp.where((labels > 0.5) & (tag < A) & inner, 1.0, 0.0)
        cacc_ref[...] += positives[:8] + positives[8:]

    weights.wait()
    begin, n, count = SPLIT[3]
    for j in range(count + 2):
        if j >= 2 and j - 2 < SPLIT[4][2]:
            for k in range(0, n, 128):
                focal_step(MARGIN + SPLIT[4][0] + (j - 2) * n + k, 128)
        if j < count:
            class_step(MARGIN + begin + j * n, n)

    def class_back(lane, n):
        here = pl.ds(lane, n)
        mains = [window(d_ref, slice(None), lane, -s, n) for s in TAPS]
        tails = [window(dt_ref, slice(None), lane, -s, n) for s in TAPS]
        inner = [interior(lane, -s, n) for s in TAPS]
        spare = jnp.zeros((8, n), F32)
        block = block_ref[:, here]
        stack = jnp.concatenate(
            mains + [jnp.concatenate(tails + [spare], axis=0).astype(BF)], axis=0
        )
        dblock = dot(w3t_ref[...], stack)
        dsum = jnp.where(block.astype(F32) > 0, dblock, 0.0).astype(BF)
        second = second_ref[:, here]
        within = interior(lane, 0, n)
        gexp_ref[...] += dot_nt(masked(second, within), dsum)
        dsecond = jnp.where(second.astype(F32) > 0, dot(wet_ref[...], dsum), 0.0)
        ds_ref[:, here] = dsecond.astype(BF)
        own = jnp.concatenate(
            [masked(m, i) for m, i in zip(mains, inner)]
            + [
                jnp.concatenate(
                    [jnp.where(i, t, 0.0) for t, i in zip(tails, inner)] + [spare], axis=0
                ).astype(BF)
            ],
            axis=0,
        )
        gclass_ref[...] += dot_nt(own, block)

    weights_back.wait()
    chunks(*SPLIT[5], class_back)

    def spatial_back(lane, n):
        stack = across(ds_ref, lane, -1, n)
        p_ref[: 3 * MID, pl.ds(lane, n)] = dot(w2t_ref[...], stack)
        own = jnp.concatenate(
            [
                masked(stack[k * MID : k * MID + MID], interior(lane, 1 - k, n))
                for k in range(3)
            ],
            axis=0,
        )
        first = jnp.concatenate(
            [window(first_ref, slice(None), lane, k * STRIDE, n) for k in (-1, 0, 1)], axis=0
        )
        gspat_ref[...] += dot_nt(own, first)

    chunks(*SPLIT[6], spatial_back)

    def first_back(lane, n):
        here = pl.ds(lane, n)
        dfirst = down(p_ref, lane, -1, MID, n)
        keep = (first_ref[:, here].astype(F32) > 0) & interior(lane, 0, n)
        dfirst = jnp.where(keep, dfirst, 0.0).astype(BF)
        gred_ref[...] += dot_nt(dfirst, x_ref[:C, here])

    chunks(*SPLIT[7], first_back)

    out_ref[:STACK] = gclass_ref[:, :128].astype(BF)
    out_ref[STACK:RED0] = gclass_ref[:, 128:].astype(BF)
    out_ref[RED0 : RED0 + MID] = gred_ref[:, :128].astype(BF)
    out_ref[RED0 + MID : SPAT0] = gred_ref[:, 128:].astype(BF)
    out_ref[SPAT0 : SPAT0 + 3 * MID] = gspat_ref[:, : 2 * MID].astype(BF)
    half = 3 * MID // 2
    out_ref[SPAT0 + 3 * MID : EXP0] = jnp.concatenate(
        [gspat_ref[:half, 2 * MID :], gspat_ref[half:, 2 * MID :]], axis=1
    ).astype(BF)
    out_ref[EXP0 : EXP0 + MID] = gexp_ref[:, :128].astype(BF)
    out_ref[EXP0 + MID : STAT0] = gexp_ref[:, 128:].astype(BF)
    out_ref[STAT0:] = jnp.zeros((DEVICES * SHARE - STAT0, 128), BF)
    focal = jnp.sum(facc_ref[...], keepdims=True)
    count = jnp.sum(cacc_ref[...], keepdims=True)
    stats = stat_rows(focal, count, 16)
    at = lax.broadcasted_iota(jnp.int32, (16, 128), 0)
    out_ref[STAT0 : STAT0 + 16] = jnp.where(at == core_ref[0], stats, 0.0).astype(BF)
    for ref, core in ((keep_ref, core_ref[0]), (send_ref, 1 - core_ref[0])):
        ref[...] = out_ref[pl.ds(pl.multiple_of(core * HALF, HALF), HALF), :]


def rounded(x):
    return x.astype(BF).astype(F32)


def stat_rows(focal, count, rows):
    lane = lax.broadcasted_iota(jnp.int32, (rows, 128), 1)
    out = jnp.zeros((rows, 128), F32)
    for at, value in ((0, focal), (3, count)):
        value = jnp.broadcast_to(value, (rows, 128))
        for k in range(3):
            piece = rounded(value)
            out = jnp.where(lane == at + k, piece, out)
            value = value - piece
    return out


def stat_values(row):
    lane = lax.broadcasted_iota(jnp.int32, row.shape, 1)
    focal = jnp.sum(jnp.where(lane < 3, row, 0.0), axis=1, keepdims=True)
    count = jnp.sum(jnp.where((lane >= 3) & (lane < 6), row, 0.0), axis=1, keepdims=True)
    return focal, count


def sum_kernel(index_ref, came_ref, copies_ref):
    total = came_ref[0].astype(F32)
    for k in range(1, PAIRS):
        total = total + came_ref[k].astype(F32)
    row = STAT0 % SHARE
    at = lax.broadcasted_iota(jnp.int32, (SHARE, 128), 0)
    focal, count = stat_values(total[row : row + 1] + total[row + 1 : row + 2])
    stats = stat_rows(focal, count, SHARE)
    total = jnp.where((at == row) & (index_ref[0] == STAT0 // SHARE), stats, total)
    total = total.astype(BF)
    for k in range(PAIRS):
        copies_ref[k] = total


def final_kernel(
    core_ref, own_ref, other_ref, loss_ref, gred_ref, gspat_ref, gexp_ref, gclass_ref, flat_ref
):
    for ref, core in ((own_ref, core_ref[0]), (other_ref, 1 - core_ref[0])):
        flat_ref[pl.ds(pl.multiple_of(core * HALF, HALF), HALF), :] = ref[...]
    focal, count = stat_values(flat_ref[STAT0 : STAT0 + 16].astype(F32)[:1])
    scale = 1.0 / count
    loss_ref[...] = focal * scale

    def rows(lo, n):
        return flat_ref[lo : lo + n].astype(F32) * scale

    for half in range(2):
        lanes = slice(half * 128, half * 128 + 128)
        tails = rows(half * STACK + 9 * 128, STACK - 9 * 128)
        for t in range(9):
            gclass_ref[t, :128, lanes] = rows(half * STACK + t * 128, 128)
            gclass_ref[t, 128:, lanes] = tails[t * TAIL : t * TAIL + 7]
        gred_ref[:, lanes] = rows(RED0 + half * MID, MID)
        gexp_ref[:, lanes] = rows(EXP0 + half * MID, MID)
    spat = rows(SPAT0, 3 * MID)
    last = rows(SPAT0 + 3 * MID, 3 * MID // 2)
    half = 3 * MID // 2
    for dx in range(3):
        for dy in range(2):
            gspat_ref[3 * dy + dx] = spat[dx * MID : dx * MID + MID, dy * MID : dy * MID + MID]
    gspat_ref[6] = last[:MID, :MID]
    gspat_ref[7, : half - MID] = last[MID:, :MID]
    gspat_ref[7, half - MID :] = last[: 2 * MID - half, MID:]
    gspat_ref[8] = last[2 * MID - half :, MID:]


def per_device(
    inputs, reduce_weight, spatial_weight, expand_weight, class_weight, anchor_labels, anchor_mask
):
    one = jnp.ones((1, ROWS, COLS), BF)
    none = jnp.zeros((TAGS - 2 * A - 1, ROWS, COLS), BF)
    tags = jnp.concatenate(
        [anchor_labels[0].astype(BF), anchor_mask[0].astype(BF), one, none], axis=0
    )

    def edge_rows(at):
        fields = jnp.concatenate([inputs[0, :, at : at + HALO], tags[:, at : at + HALO]], axis=0)
        return jnp.transpose(fields, (1, 0, 2))

    ahead = [(i, i + 1) for i in range(3)]
    back = [(i + 1, i) for i in range(3)]
    top = lax.ppermute(edge_rows(ROWS - HALO), "row", ahead)
    bottom = lax.ppermute(edge_rows(0), "row", back)
    maps = jnp.transpose(inputs[0], (1, 0, 2))
    tags = jnp.transpose(tags, (1, 0, 2))
    params = pltpu.CompilerParams(vmem_limit_bytes=56 << 20)
    pack = jax.ShapeDtypeStruct((CHANNELS, 128), BF)
    start = jax.ShapeDtypeStruct((CHANNELS, WIDTH), BF)
    left_edge, right_edge, start = pl.pallas_call(
        edges_kernel, out_shape=(pack, pack, start), compiler_params=params
    )(maps, tags)
    pack = jax.ShapeDtypeStruct((CHANNELS, 256), BF)
    left_edge, right_edge = pl.pallas_call(
        corners_kernel, out_shape=(pack, pack), compiler_params=params
    )(left_edge, right_edge, top, bottom)
    left = lax.ppermute(right_edge, "col", ahead)
    right = lax.ppermute(left_edge, "col", back)

    w2 = jnp.transpose(spatial_weight, (0, 2, 1, 3)).reshape(3 * MID, 3 * MID)
    w2t = jnp.transpose(spatial_weight, (0, 3, 1, 2)).reshape(3 * MID, 3 * MID)
    w3 = jnp.pad(class_weight, ((0, 0), (0, 0), (0, 136 - OUT), (0, 0)))
    w3 = jnp.transpose(w3, (0, 2, 1, 3)).reshape(3 * 136, 3 * C)
    w9 = class_weight.reshape(9, OUT, C)
    w3t = jnp.concatenate(
        [
            w9[:, :128].reshape(9 * 128, C),
            jnp.pad(w9[:, 128:], ((0, 0), (0, TAIL - 7), (0, 0))).reshape(9 * TAIL, C),
            jnp.zeros((8, C), BF),
        ],
        axis=0,
    ).T
    spread = np.zeros((136, CHANNELS - C), np.float32)
    for o in range(OUT):
        spread[o, o // K] = 1.0
        spread[o, A + o // K] = 16.0
    spread = jnp.asarray(spread, BF)

    shape = jax.ShapeDtypeStruct
    core = lax.axis_index("core").astype(jnp.int32).reshape(1)
    keep, send = pl.pallas_call(
        main_kernel,
        out_shape=(shape((HALF, 128), BF), shape((HALF, 128), BF)),
        in_specs=[pl.BlockSpec(memory_space=pltpu.SMEM), pl.BlockSpec(memory_space=pl.ANY)]
        + [pl.BlockSpec(memory_space=pltpu.VMEM)] * 9
        + [pl.BlockSpec(memory_space=pl.ANY)] * 2
        + [pl.BlockSpec(memory_space=pltpu.VMEM)],
        scratch_shapes=[
            pltpu.VMEM((CHANNELS, WIDTH), BF),
            pltpu.VMEM((MID, WIDTH), BF),
            pltpu.VMEM((MID, WIDTH), BF),
            pltpu.VMEM((C, WIDTH), BF),
            pltpu.VMEM((128, WIDTH), BF),
            pltpu.VMEM((TAIL, WIDTH), F32),
            pltpu.VMEM((MID, WIDTH), BF),
            pltpu.VMEM((3 * 136, WIDTH), F32),
            pltpu.VMEM((8, 128), F32),
            pltpu.VMEM((8, 128), F32),
            pltpu.VMEM((STACK, C), F32),
            pltpu.VMEM((MID, C), F32),
            pltpu.VMEM((3 * MID, 3 * MID), F32),
            pltpu.VMEM((MID, C), F32),
            pltpu.VMEM((DEVICES * SHARE, 128), BF),
            pltpu.VMEM((3 * 136, 3 * C), BF),
            pltpu.VMEM((C, STACK), BF),
            pltpu.SemaphoreType.DMA((3,)),
        ],
        compiler_params=params,
    )(
        core, start, top, bottom, left, right,
        reduce_weight, w2, w2t, expand_weight, expand_weight.T, w3, w3t, spread,
    )

    swap = [(0, 1), (1, 0)]
    pair = lax.ppermute(send, "core", swap).astype(F32) + keep.astype(F32)
    came = lax.all_to_all(pair.astype(BF).reshape(PAIRS, SHARE, 128), CHIPS, 0, 0, tiled=True)
    index = core * PAIRS + lax.axis_index(CHIPS).astype(jnp.int32)
    copies = pl.pallas_call(
        sum_kernel,
        out_shape=shape((PAIRS, SHARE, 128), BF),
        in_specs=[
            pl.BlockSpec(memory_space=pltpu.SMEM),
            pl.BlockSpec(memory_space=pltpu.VMEM),
        ],
        compiler_params=params,
    )(index, came)
    own = lax.all_to_all(copies, CHIPS, 0, 0, tiled=True).reshape(PAIRS * SHARE, 128)
    other = lax.ppermute(own, "core", swap)
    loss, gred, gspat, gexp, gclass = pl.pallas_call(
        final_kernel,
        out_shape=(
            shape((1, 1), F32),
            shape((MID, C), F32),
            shape((9, MID, MID), F32),
            shape((MID, C), F32),
            shape((9, OUT, C), F32),
        ),
        in_specs=[pl.BlockSpec(memory_space=pltpu.SMEM)]
        + [pl.BlockSpec(memory_space=pltpu.VMEM)] * 2,
        scratch_shapes=[pltpu.VMEM((DEVICES * SHARE, 128), BF)],
        compiler_params=params,
    )(core, own, other)
    return (
        loss.reshape(()),
        gred,
        gspat.reshape(3, 3, MID, MID),
        gexp.T,
        gclass.reshape(3, 3, OUT, C),
    )


def solution(mesh):
    finer = Mesh(
        mesh.devices.reshape(4, 2, mesh.shape["row"], mesh.shape["col"]),
        ("y", "core", "row", "col"),
    )
    maps = P(("y", "core"), None, "row", "col")
    return jax.shard_map(
        per_device,
        mesh=finer,
        in_specs=(maps, P(), P(), P(), P(), maps, maps),
        out_specs=(P(), P(), P(), P(), P()),
        check_vma=False,
    )
```

```python
import jax
import jax.numpy as jnp
import numpy as np
from jax import lax
from jax.experimental import pallas as pl
from jax.experimental.pallas import tpu as pltpu
from jax.sharding import Mesh
from jax.sharding import PartitionSpec as P

A = 9
K = 15
OUT = A * K
C = 256
MID = 64
HALO = 4
ROWS = 32
COLS = 128
FULL = ROWS + 2 * HALO
STRIDE = COLS + 2 * HALO
CHANNELS = 288
MARGIN = 256
WIDTH = 6656
RIGHT = MARGIN + 5120
PIPE = 640
SPLIT = (
    (0, 5632, 1),
    (0, 5632, 1),
    (128, 5376, 1),
    (0, PIPE, 9),
    (256, PIPE, 8),
    (384, 2432, 2),
    (384, 4864, 1),
    (512, 4608, 1),
)
LABEL0 = C
MASK0 = C + A
ONE0 = C + 2 * A
TAGS = CHANNELS - C
TAIL = 8
STACK = 9 * 128 + 9 * TAIL + 8
CHIPS = ("y", "row", "col")
DEVICES = 128
PAIRS = 64
SHARE = 24
HALF = PAIRS * SHARE
RED0 = 2 * STACK
SPAT0 = RED0 + 2 * MID
EXP0 = SPAT0 + 9 * MID // 2
STAT0 = EXP0 + C // 2
TAPS = [(dy - 1) * STRIDE + (dx - 1) for dy in range(3) for dx in range(3)]
BF = jnp.bfloat16
F32 = jnp.float32


def put(ref, rows, tile, value, lo, hi):
    lane = lax.broadcasted_iota(jnp.int32, value.shape, 1)
    where = slice(tile * 128, tile * 128 + 128)
    ref[rows, where] = jnp.where((lane >= lo) & (lane < hi), value, ref[rows, where])


BODY = slice(0, C)
REST = slice(C, CHANNELS)
BOTH = slice(0, CHANNELS)


def place(ref, rows, source, r):
    at = MARGIN + r * STRIDE + HALO
    turn, tile = (at % 128, at // 128)
    turned = pltpu.roll(source, turn, 1)
    put(ref, rows, tile, turned, turn, 128)
    put(ref, rows, tile + 1, turned, 0, turn)


def put_span(ref, value, at, width):
    tile, low = divmod(at, 128)
    put(ref, BOTH, tile, value, low, min(low + width, 128))
    if low + width > 128:
        put(ref, BOTH, tile + 1, value, 0, low + width - 128)


def spot(r):
    if HALO <= r < HALO + ROWS:
        return HALO * (r - HALO)
    return 128 + HALO * (r if r < HALO else r - ROWS)


def edges_kernel(maps_ref, tags_ref, left_ref, right_ref, x_ref):
    x_ref[...] = jnp.zeros_like(x_ref)
    left_ref[...] = jnp.zeros_like(left_ref)
    right_ref[...] = jnp.zeros_like(right_ref)
    for r in range(ROWS):
        at = HALO * r
        for rows, source in ((BODY, maps_ref[r]), (REST, tags_ref[r])):
            put(left_ref, rows, 0, pltpu.roll(source, at, 1), at, at + HALO)
            put(right_ref, rows, 0, pltpu.roll(source, (at + HALO) % 128, 1), at, at + HALO)
            place(x_ref, rows, source, r + HALO)


def corners_kernel(left_ref, right_ref, top_ref, bottom_ref, wide_left_ref, wide_right_ref):
    for edge_ref, wide_ref in ((left_ref, wide_left_ref), (right_ref, wide_right_ref)):
        wide_ref[:, :128] = edge_ref[...]
        wide_ref[:, 128:] = jnp.zeros_like(edge_ref)
    for h in range(2 * HALO):
        source = top_ref[h] if h < HALO else bottom_ref[h - HALO]
        at = HALO * h
        put(wide_left_ref, BOTH, 1, pltpu.roll(source, at, 1), at, at + HALO)
        put(wide_right_ref, BOTH, 1, pltpu.roll(source, at + HALO, 1), at, at + HALO)


def aligned(lane):
    return lane if isinstance(lane, int) else pl.multiple_of(lane, 128)


def window(ref, rows, lane, shift, n):
    base = (shift // 128) * 128
    turn = shift - base
    if turn == 0:
        return ref[rows, pl.ds(aligned(lane + base), n)]
    wide = ref[rows, pl.ds(aligned(lane + base), n + 128)]
    return pltpu.roll(wide, n + 128 - turn, 1)[:, :n]


def interior(lane, shift, n):
    p = lane - MARGIN + shift + lax.broadcasted_iota(jnp.int32, (1, n), 1)
    r = (p * 30841) >> 22
    c = p - r * STRIDE
    return (r >= HALO) & (r < HALO + ROWS) & (c >= HALO) & (c < HALO + COLS)


def masked(value, mask):
    return value * jnp.where(mask, 1.0, 0.0).astype(BF)


def dot(a, b):
    return jnp.dot(a, b, preferred_element_type=F32)


def dot_nt(a, b):
    return lax.dot_general(a, b, (((1,), (1,)), ((), ())), preferred_element_type=F32)


def chunks(start, n, count, body):
    def step(j, carry):
        body(pl.multiple_of(MARGIN + start + j * n, 128), n)
        return carry

    lax.fori_loop(0, count, step, 0)


def across(ref, lane, sign, n):
    return jnp.concatenate([window(ref, slice(None), lane, sign * k, n) for k in (-1, 0, 1)], axis=0)


def down(ref, lane, sign, size, n):
    parts = [
        window(ref, slice(k * size, k * size + size), lane, sign * (k - 1) * STRIDE, n)
        for k in range(3)
    ]
    return parts[0] + parts[1] + parts[2]


def main_kernel(
    core_ref, x0_ref, top_ref, bottom_ref, left_ref, right_ref,
    wr_ref, w2_ref, w2t_ref, we_ref, wet_ref, w3_raw, w3t_raw, e_ref,
    keep_ref, send_ref,
    x_ref, first_ref, second_ref, block_ref, d_ref, dt_ref, ds_ref, p_ref, facc_ref, cacc_ref,
    gclass_ref, gred_ref, gspat_ref, gexp_ref, out_ref, w3_ref, w3t_ref, sem,
):
    copy = pltpu.make_async_copy(x0_ref, x_ref, sem.at[0])
    weights = pltpu.make_async_copy(w3_raw, w3_ref, sem.at[1])
    weights_back = pltpu.make_async_copy(w3t_raw, w3t_ref, sem.at[2])
    for each in (copy, weights, weights_back):
        each.start()
    p_ref[:, :MARGIN] = jnp.zeros((p_ref.shape[0], MARGIN), F32)
    for ref in (first_ref, second_ref, block_ref, d_ref, dt_ref, ds_ref):
        ref[:, : 2 * MARGIN] = jnp.zeros((ref.shape[0], 2 * MARGIN), ref.dtype)
        ref[:, RIGHT:] = jnp.zeros((ref.shape[0], WIDTH - RIGHT), ref.dtype)
    for ref in (gclass_ref, gred_ref, gspat_ref, gexp_ref, facc_ref, cacc_ref):
        ref[...] = jnp.zeros_like(ref)
    copy.wait()
    for h in range(HALO):
        place(x_ref, BOTH, top_ref[h], h)
        place(x_ref, BOTH, bottom_ref[h], h + HALO + ROWS)
    lane = lax.broadcasted_iota(jnp.int32, (CHANNELS, 128), 1)
    for r in range(-1, FULL):
        at = MARGIN + r * STRIDE + HALO + COLS
        if 0 <= r < FULL - 1 and spot(r + 1) == spot(r) + HALO:
            tile, low = divmod(spot(r), 128)
            where = slice(tile * 128, tile * 128 + 128)
            both = jnp.where(lane < low + HALO, right_ref[:, where], left_ref[:, where])
            put_span(x_ref, pltpu.roll(both, (at - low) % 128, 1), at, 2 * HALO)
            continue
        for ref, row, to in ((right_ref, r, at), (left_ref, r + 1, at + HALO)):
            if 0 <= row < FULL:
                tile, low = divmod(spot(row), 128)
                one = ref[:, tile * 128 : tile * 128 + 128]
                put_span(x_ref, pltpu.roll(one, (to - low) % 128, 1), to, HALO)

    def first_step(lane, n):
        x = x_ref[:C, pl.ds(lane, n)]
        first_ref[:, pl.ds(lane, n)] = jnp.maximum(dot(wr_ref[...], x), 0.0).astype(BF)

    chunks(*SPLIT[0], first_step)

    def spatial_step(lane, n):
        p_ref[: 3 * MID, pl.ds(lane, n)] = dot(w2_ref[...], across(first_ref, lane, 1, n))

    chunks(*SPLIT[1], spatial_step)

    def block_step(lane, n):
        here = pl.ds(lane, n)
        second = jnp.maximum(down(p_ref, lane, 1, MID, n), 0.0)
        inside = x_ref[ONE0 - 2 : ONE0 + 14, here].astype(F32)[2:3]
        second = jnp.where(inside > 0.5, second, 0.0).astype(BF)
        second_ref[:, here] = second
        total = x_ref[:C, here].astype(F32) + dot(we_ref[...], second)
        block_ref[:, here] = jnp.maximum(total, 0.0).astype(BF)

    chunks(*SPLIT[2], block_step)

    def class_step(lane, n):
        p_ref[:, pl.ds(lane, n)] = dot(w3_ref[...], across(block_ref, lane, 1, n))

    channel = lax.broadcasted_iota(jnp.int32, (136, 1), 0)
    wanted = (channel - 15 * ((channel * 4370) >> 16) + 17).astype(F32)

    def focal_step(lane, n):
        here = pl.ds(lane, n)
        z = down(p_ref, lane, 1, 136, n)
        tags = x_ref[C:CHANNELS, here]
        code = dot(e_ref[...], tags)
        target = code == wanted
        counted = code > 15.5
        u = jnp.where(target, z, -z)
        alpha = jnp.where(target, 0.25, 0.75)
        e = jnp.exp(-jnp.abs(u))
        d = 1.0 / (1.0 + e)
        ed = e * d
        positive = u >= 0
        p = jnp.where(positive, ed, d)
        q = jnp.where(positive, d, ed)
        ls = jnp.minimum(u, 0.0) - jnp.log1p(e)
        ap2 = jnp.where(counted, alpha, 0.0) * p * p
        grad = ap2 * (2.0 * q * ls - p)
        grad = jnp.where(target, grad, -grad)
        d_ref[:, here] = grad[:128].astype(BF)
        dt_ref[:, here] = grad[128:].astype(BF).astype(F32)
        inner = interior(lane, 0, n)
        focal = jnp.where(inner, ap2 * ls, 0.0)
        facc_ref[...] -= jnp.sum(focal.reshape(17, 8, n), axis=0)
        labels = tags[:16].astype(F32)
        tag = lax.broadcasted_iota(jnp.int32, (16, n), 0)
        positives = jnp.where((labels > 0.5) & (tag < A) & inner, 1.0, 0.0)
        cacc_ref[...] += positives[:8] + positives[8:]

    weights.wait()
    begin, n, count = SPLIT[3]
    for j in range(count + 2):
        if j >= 2 and j - 2 < SPLIT[4][2]:
            for k in range(0, n, 128):
                focal_step(MARGIN + SPLIT[4][0] + (j - 2) * n + k, 128)
        if j < count:
            class_step(MARGIN + begin + j * n, n)

    def class_back(lane, n):
        here = pl.ds(lane, n)
        mains = [window(d_ref, slice(None), lane, -s, n) for s in TAPS]
        tails = [window(dt_ref, slice(None), lane, -s, n) for s in TAPS]
        inner = [interior(lane, -s, n) for s in TAPS]
        spare = jnp.zeros((8, n), F32)
        block = block_ref[:, here]
        stack = jnp.concatenate(
            mains + [jnp.concatenate(tails + [spare], axis=0).astype(BF)], axis=0
        )
        dblock = dot(w3t_ref[...], stack)
        dsum = jnp.where(block.astype(F32) > 0, dblock, 0.0).astype(BF)
        second = second_ref[:, here]
        within = interior(lane, 0, n)
        gexp_ref[...] += dot_nt(masked(second, within), dsum)
        dsecond = jnp.where(second.astype(F32) > 0, dot(wet_ref[...], dsum), 0.0)
        ds_ref[:, here] = dsecond.astype(BF)
        own = jnp.concatenate(
            [masked(m, i) for m, i in zip(mains, inner)]
            + [
                jnp.concatenate(
                    [jnp.where(i, t, 0.0) for t, i in zip(tails, inner)] + [spare], axis=0
                ).astype(BF)
            ],
            axis=0,
        )
        gclass_ref[...] += dot_nt(own, block)

    weights_back.wait()
    chunks(*SPLIT[5], class_back)

    def spatial_back(lane, n):
        stack = across(ds_ref, lane, -1, n)
        p_ref[: 3 * MID, pl.ds(lane, n)] = dot(w2t_ref[...], stack)
        own = jnp.concatenate(
            [
                masked(stack[k * MID : k * MID + MID], interior(lane, 1 - k, n))
                for k in range(3)
            ],
            axis=0,
        )
        first = jnp.concatenate(
            [window(first_ref, slice(None), lane, k * STRIDE, n) for k in (-1, 0, 1)], axis=0
        )
        gspat_ref[...] += dot_nt(own, first)

    chunks(*SPLIT[6], spatial_back)

    def first_back(lane, n):
        here = pl.ds(lane, n)
        dfirst = down(p_ref, lane, -1, MID, n)
        keep = (first_ref[:, here].astype(F32) > 0) & interior(lane, 0, n)
        dfirst = jnp.where(keep, dfirst, 0.0).astype(BF)
        gred_ref[...] += dot_nt(dfirst, x_ref[:C, here])

    chunks(*SPLIT[7], first_back)

    out_ref[:STACK] = gclass_ref[:, :128].astype(BF)
    out_ref[STACK:RED0] = gclass_ref[:, 128:].astype(BF)
    out_ref[RED0 : RED0 + MID] = gred_ref[:, :128].astype(BF)
    out_ref[RED0 + MID : SPAT0] = gred_ref[:, 128:].astype(BF)
    out_ref[SPAT0 : SPAT0 + 3 * MID] = gspat_ref[:, : 2 * MID].astype(BF)
    half = 3 * MID // 2
    out_ref[SPAT0 + 3 * MID : EXP0] = jnp.concatenate(
        [gspat_ref[:half, 2 * MID :], gspat_ref[half:, 2 * MID :]], axis=1
    ).astype(BF)
    out_ref[EXP0 : EXP0 + MID] = gexp_ref[:, :128].astype(BF)
    out_ref[EXP0 + MID : STAT0] = gexp_ref[:, 128:].astype(BF)
    out_ref[STAT0:] = jnp.zeros((DEVICES * SHARE - STAT0, 128), BF)
    focal = jnp.sum(facc_ref[...], keepdims=True)
    count = jnp.sum(cacc_ref[...], keepdims=True)
    stats = stat_rows(focal, count, 16)
    at = lax.broadcasted_iota(jnp.int32, (16, 128), 0)
    out_ref[STAT0 : STAT0 + 16] = jnp.where(at == core_ref[0], stats, 0.0).astype(BF)
    for ref, core in ((keep_ref, core_ref[0]), (send_ref, 1 - core_ref[0])):
        ref[...] = out_ref[pl.ds(pl.multiple_of(core * HALF, HALF), HALF), :]


def rounded(x):
    return x.astype(BF).astype(F32)


def stat_rows(focal, count, rows):
    lane = lax.broadcasted_iota(jnp.int32, (rows, 128), 1)
    out = jnp.zeros((rows, 128), F32)
    for at, value in ((0, focal), (3, count)):
        value = jnp.broadcast_to(value, (rows, 128))
        for k in range(3):
            piece = rounded(value)
            out = jnp.where(lane == at + k, piece, out)
            value = value - piece
    return out


def stat_values(row):
    lane = lax.broadcasted_iota(jnp.int32, row.shape, 1)
    focal = jnp.sum(jnp.where(lane < 3, row, 0.0), axis=1, keepdims=True)
    count = jnp.sum(jnp.where((lane >= 3) & (lane < 6), row, 0.0), axis=1, keepdims=True)
    return focal, count


def sum_kernel(index_ref, came_ref, copies_ref):
    total = came_ref[0].astype(F32)
    for k in range(1, PAIRS):
        total = total + came_ref[k].astype(F32)
    row = STAT0 % SHARE
    at = lax.broadcasted_iota(jnp.int32, (SHARE, 128), 0)
    focal, count = stat_values(total[row : row + 1] + total[row + 1 : row + 2])
    stats = stat_rows(focal, count, SHARE)
    total = jnp.where((at == row) & (index_ref[0] == STAT0 // SHARE), stats, total)
    total = total.astype(BF)
    for k in range(PAIRS):
        copies_ref[k] = total


def final_kernel(
    core_ref, own_ref, other_ref, loss_ref, gred_ref, gspat_ref, gexp_ref, gclass_ref, flat_ref
):
    for ref, core in ((own_ref, core_ref[0]), (other_ref, 1 - core_ref[0])):
        flat_ref[pl.ds(pl.multiple_of(core * HALF, HALF), HALF), :] = ref[...]
    focal, count = stat_values(flat_ref[STAT0 : STAT0 + 16].astype(F32)[:1])
    scale = 1.0 / count
    loss_ref[...] = focal * scale

    def rows(lo, n):
        return flat_ref[lo : lo + n].astype(F32) * scale

    for half in range(2):
        lanes = slice(half * 128, half * 128 + 128)
        tails = rows(half * STACK + 9 * 128, STACK - 9 * 128)
        for t in range(9):
            gclass_ref[t, :128, lanes] = rows(half * STACK + t * 128, 128)
            gclass_ref[t, 128:, lanes] = tails[t * TAIL : t * TAIL + 7]
        gred_ref[:, lanes] = rows(RED0 + half * MID, MID)
        gexp_ref[:, lanes] = rows(EXP0 + half * MID, MID)
    spat = rows(SPAT0, 3 * MID)
    last = rows(SPAT0 + 3 * MID, 3 * MID // 2)
    half = 3 * MID // 2
    for dx in range(3):
        for dy in range(2):
            gspat_ref[3 * dy + dx] = spat[dx * MID : dx * MID + MID, dy * MID : dy * MID + MID]
    gspat_ref[6] = last[:MID, :MID]
    gspat_ref[7, : half - MID] = last[MID:, :MID]
    gspat_ref[7, half - MID :] = last[: 2 * MID - half, MID:]
    gspat_ref[8] = last[2 * MID - half :, MID:]


def per_device(
    inputs, reduce_weight, spatial_weight, expand_weight, class_weight, anchor_labels, anchor_mask
):
    one = jnp.ones((1, ROWS, COLS), BF)
    none = jnp.zeros((TAGS - 2 * A - 1, ROWS, COLS), BF)
    tags = jnp.concatenate(
        [anchor_labels[0].astype(BF), anchor_mask[0].astype(BF), one, none], axis=0
    )

    def edge_rows(at):
        fields = jnp.concatenate([inputs[0, :, at : at + HALO], tags[:, at : at + HALO]], axis=0)
        return jnp.transpose(fields, (1, 0, 2))

    ahead = [(i, i + 1) for i in range(3)]
    back = [(i + 1, i) for i in range(3)]
    top = lax.ppermute(edge_rows(ROWS - HALO), "row", ahead)
    bottom = lax.ppermute(edge_rows(0), "row", back)
    maps = jnp.transpose(inputs[0], (1, 0, 2))
    tags = jnp.transpose(tags, (1, 0, 2))
    params = pltpu.CompilerParams(vmem_limit_bytes=56 << 20)
    pack = jax.ShapeDtypeStruct((CHANNELS, 128), BF)
    start = jax.ShapeDtypeStruct((CHANNELS, WIDTH), BF)
    left_edge, right_edge, start = pl.pallas_call(
        edges_kernel, out_shape=(pack, pack, start), compiler_params=params
    )(maps, tags)
    pack = jax.ShapeDtypeStruct((CHANNELS, 256), BF)
    left_edge, right_edge = pl.pallas_call(
        corners_kernel, out_shape=(pack, pack), compiler_params=params
    )(left_edge, right_edge, top, bottom)
    left = lax.ppermute(right_edge, "col", ahead)
    right = lax.ppermute(left_edge, "col", back)

    w2 = jnp.transpose(spatial_weight, (0, 2, 1, 3)).reshape(3 * MID, 3 * MID)
    w2t = jnp.transpose(spatial_weight, (0, 3, 1, 2)).reshape(3 * MID, 3 * MID)
    w3 = jnp.pad(class_weight, ((0, 0), (0, 0), (0, 136 - OUT), (0, 0)))
    w3 = jnp.transpose(w3, (0, 2, 1, 3)).reshape(3 * 136, 3 * C)
    w9 = class_weight.reshape(9, OUT, C)
    w3t = jnp.concatenate(
        [
            w9[:, :128].reshape(9 * 128, C),
            jnp.pad(w9[:, 128:], ((0, 0), (0, TAIL - 7), (0, 0))).reshape(9 * TAIL, C),
            jnp.zeros((8, C), BF),
        ],
        axis=0,
    ).T
    spread = np.zeros((136, CHANNELS - C), np.float32)
    for o in range(OUT):
        spread[o, o // K] = 1.0
        spread[o, A + o // K] = 16.0
    spread = jnp.asarray(spread, BF)

    shape = jax.ShapeDtypeStruct
    core = lax.axis_index("core").astype(jnp.int32).reshape(1)
    keep, send = pl.pallas_call(
        main_kernel,
        out_shape=(shape((HALF, 128), BF), shape((HALF, 128), BF)),
        in_specs=[pl.BlockSpec(memory_space=pltpu.SMEM), pl.BlockSpec(memory_space=pl.ANY)]
        + [pl.BlockSpec(memory_space=pltpu.VMEM)] * 9
        + [pl.BlockSpec(memory_space=pl.ANY)] * 2
        + [pl.BlockSpec(memory_space=pltpu.VMEM)],
        scratch_shapes=[
            pltpu.VMEM((CHANNELS, WIDTH), BF),
            pltpu.VMEM((MID, WIDTH), BF),
            pltpu.VMEM((MID, WIDTH), BF),
            pltpu.VMEM((C, WIDTH), BF),
            pltpu.VMEM((128, WIDTH), BF),
            pltpu.VMEM((TAIL, WIDTH), F32),
            pltpu.VMEM((MID, WIDTH), BF),
            pltpu.VMEM((3 * 136, WIDTH), F32),
            pltpu.VMEM((8, 128), F32),
            pltpu.VMEM((8, 128), F32),
            pltpu.VMEM((STACK, C), F32),
            pltpu.VMEM((MID, C), F32),
            pltpu.VMEM((3 * MID, 3 * MID), F32),
            pltpu.VMEM((MID, C), F32),
            pltpu.VMEM((DEVICES * SHARE, 128), BF),
            pltpu.VMEM((3 * 136, 3 * C), BF),
            pltpu.VMEM((C, STACK), BF),
            pltpu.SemaphoreType.DMA((3,)),
        ],
        compiler_params=params,
    )(
        core, start, top, bottom, left, right,
        reduce_weight, w2, w2t, expand_weight, expand_weight.T, w3, w3t, spread,
    )

    swap = [(0, 1), (1, 0)]
    pair = lax.ppermute(send, "core", swap).astype(F32) + keep.astype(F32)
    came = lax.all_to_all(pair.astype(BF).reshape(PAIRS, SHARE, 128), CHIPS, 0, 0, tiled=True)
    index = core * PAIRS + lax.axis_index(CHIPS).astype(jnp.int32)
    copies = pl.pallas_call(
        sum_kernel,
        out_shape=shape((PAIRS, SHARE, 128), BF),
        in_specs=[
            pl.BlockSpec(memory_space=pltpu.SMEM),
            pl.BlockSpec(memory_space=pltpu.VMEM),
        ],
        compiler_params=params,
    )(index, came)
    own = lax.all_to_all(copies, CHIPS, 0, 0, tiled=True).reshape(PAIRS * SHARE, 128)
    other = lax.ppermute(own, "core", swap)
    loss, gred, gspat, gexp, gclass = pl.pallas_call(
        final_kernel,
        out_shape=(
            shape((1, 1), F32),
            shape((MID, C), F32),
            shape((9, MID, MID), F32),
            shape((MID, C), F32),
            shape((9, OUT, C), F32),
        ),
        in_specs=[pl.BlockSpec(memory_space=pltpu.SMEM)]
        + [pl.BlockSpec(memory_space=pltpu.VMEM)] * 2,
        scratch_shapes=[pltpu.VMEM((DEVICES * SHARE, 128), BF)],
        compiler_params=params,
    )(core, own, other)
    return (
        loss.reshape(()),
        gred,
        gspat.reshape(3, 3, MID, MID),
        gexp.T,
        gclass.reshape(3, 3, OUT, C),
    )


def solution(mesh):
    finer = Mesh(
        mesh.devices.reshape(4, 2, mesh.shape["row"], mesh.shape["col"]),
        ("y", "core", "row", "col"),
    )
    maps = P(("y", "core"), None, "row", "col")
    return jax.shard_map(
        per_device,
        mesh=finer,
        in_specs=(maps, P(), P(), P(), P(), maps, maps),
        out_specs=(P(), P(), P(), P(), P()),
        check_vma=False,
    )
```
